256 devices in a mesh: ctx: 32 (over x, z), grp: 8 (over y, core).
Axes of the slice: x: 4, y: 4, z: 8, core: 2. Of those that a mesh axis runs over, the one named last changes fastest.
Arguments:
- out_grad: bfloat16 [16384, 2048], P('ctx', 'grp'), may hold values from -6 to 6
- filter_mats: bfloat16 [16, 2048, 2048], P('grp', 'ctx'), may hold values from -0.125 to 0.125
- coeffs: float32 [16, 80], replicated, may hold values from -0.15625 to 0.15625
- pole_rates: float32 [80], replicated, may hold values from 1.2207031e-06 to 0.03
Outputs:
- in_grad: bfloat16 [16384, 2048], P('ctx', 'grp')
The draws below stay inside these ranges and needn't reach their ends.
All inputs are finite; a program needn't handle non-finite values.
Results may differ from the reference program's by a relative error of at most 0.001.
Values may be sent and summed in bfloat16 or wider, within the bound.
A program may use at most 128 MiB of HBM per device.

```python
import math
import jax
import jax.numpy as jnp
from jax import lax

D = 2048
K = 16
P_SIZE = 80
TOK_DEV = 512
TOKENS = 16384
N_CTX = 32


def block_scale(rng, extent, cuts, smallest, high):
    loudness, own = 1.0, jax.random.fold_in(rng, 6)
    for axis_at, blocks in cuts:
        steps = jnp.exp(jax.random.uniform(jax.random.fold_in(own, axis_at), (blocks,), jnp.float32, smallest / len(cuts), high / len(cuts)))
        loudness = loudness * jnp.repeat(steps, extent[axis_at] // blocks).reshape([-1 if axis == axis_at else 1 for axis in range(len(extent))])
    return loudness


def bell_draw(rng, extent, spread, most, shards=(), kind=jnp.bfloat16):
    loudness = block_scale(rng, extent, shards, -0.22, 0.18) if shards else 1.0
    values = jax.random.normal(rng, extent, jnp.float32) * spread * loudness
    return jnp.minimum(jnp.maximum(values, -most), most).astype(kind)


def setup_inputs(seed: int = 0) -> dict:
    arg_keys = jax.random.split(jax.random.key(seed), 5)
    return {
        "out_grad": bell_draw(arg_keys[0], (TOKENS, D), 1.0, 6.0, ((0, 32), (1, 8))),
        "filter_mats": bell_draw(arg_keys[1], (K, D, D), D ** -0.5, 0.125, ((0, 8), (1, 32))),
        "coeffs": bell_draw(arg_keys[2], (K, P_SIZE), (K * P_SIZE) ** -0.5, 0.15625, (), jnp.float32),
        "pole_rates": jnp.clip(jnp.exp(jax.random.uniform(arg_keys[3], (P_SIZE,), jnp.float32, math.log(1.220703097715159e-06), math.log(0.03))), 1.220703097715159e-06, 0.03),
    }


def reference(out_grad, filter_mats, coeffs, pole_rates):
    exact_prec = lax.Precision.HIGHEST
    pole_gains = jnp.sqrt(-jnp.expm1(-2.0 * pole_rates))
    positions = jnp.arange(TOK_DEV).astype(jnp.float32)
    lag_mat = positions[:, None] - positions[None, :]
    causal = lag_mat >= 0.0
    lag_pos = jnp.where(causal, lag_mat, jnp.float32(0.0))
    scaled = coeffs * pole_gains[None, :]

    def kernel_one(coef_row):
        values = lax.optimization_barrier(jnp.sum(coef_row[:, None, None] * jnp.exp(-pole_rates[:, None, None] * lag_pos[None]), axis=0))
        return jnp.where(causal, values, jnp.float32(0.0))
    kernel_mat = lax.map(kernel_one, scaled)
    decay_pos = jnp.exp(-positions[:, None] * pole_rates[None, :])
    weights = coeffs[:, :, None] * decay_pos.T[None]
    edge_decay = pole_gains[None, :] * jnp.exp(-(TOK_DEV - positions)[:, None] * pole_rates[None, :])
    block_decay = jnp.exp(-TOK_DEV * pole_rates)[:, None]
    mats_wide = filter_mats.astype(jnp.float32)
    blocks = out_grad.reshape(N_CTX, TOK_DEV, D)

    def advance(carried, grad_block):
        proj_grad = jnp.einsum('tj,kij->kti', grad_block.astype(jnp.float32), mats_wide, precision=exact_prec)
        near_part = jnp.einsum('kts,kti->si', kernel_mat, proj_grad, precision=exact_prec)
        far_part = jnp.dot(edge_decay, carried, precision=exact_prec)
        result = (near_part + far_part).astype(jnp.bfloat16)
        updated = jnp.einsum('kpt,kti->pi', weights, proj_grad, precision=exact_prec) + block_decay * carried
        return (updated, result)
    start_state = jnp.zeros((P_SIZE, D), jnp.float32)
    final_state, results = lax.scan(advance, start_state, blocks, reverse=True)
    return results.reshape(TOKENS, D)
```

```python
import jax
import jax.numpy as jnp
from jax import lax
from jax.experimental import pallas as pl
from jax.experimental.pallas import tpu as pltpu
from jax.sharding import PartitionSpec as P

MESH = pl.DeviceIdType.MESH
F32, BF16 = jnp.float32, jnp.bfloat16
NX, NZ, NY = 4, 8, 4
TOK, WIDE, HALF, D = 512, 256, 1024, 2048
POLES, UNITS = 80, 24
HI = TOK
LO = TOK + POLES
ROWS = TOK + 2 * POLES
NT = (((1,), (1,)), ((), ()))
NN = (((1,), (0,)), ((), ()))


def split(value):
    high = value.astype(BF16)
    return high, (value - high.astype(F32)).astype(BF16)


def mm(a, b, dims=NN):
    return lax.dot_general(a, b, dims, preferred_element_type=F32)


def kernel(
    g_ref, m_ref, rates_col, rates_row, gains_row, coef_row, out_ref,
    grads, mats, kern_hi, kern_lo, proj_hi, proj_lo, parts, arrived, edge_hi, edge_lo,
    state_hi, state_lo, coef_col, unit_rates, unit_out, unit_in, total_out, total_in,
    enter_out, enter_in,
    g_send, g_recv, gs_send, gs_recv, m_send, m_recv, ms_send, ms_recv, u_send, u_recv,
    t_send, t_recv, e_send, e_recv, o_send, o_recv, l_sem,
):
    ctx, grp = lax.axis_index("ctx"), lax.axis_index("grp")
    x, z, y, c = ctx // NZ, ctx % NZ, grp // 2, grp % 2

    def device(x_to=None, z_to=None, y_to=None, c_to=None):
        pick = lambda new, own: own if new is None else new
        return (pick(x_to, x) * NZ + pick(z_to, z), pick(y_to, y) * 2 + pick(c_to, c))

    def remote(src, dst, send, recv, target):
        copy = pltpu.make_async_remote_copy(
            src_ref=src, dst_ref=dst, send_sem=send, recv_sem=recv,
            device_id=target, device_id_type=MESH,
        )
        return copy

    sibling = device(c_to=1 - c)
    slot = lambda x_of: (x_of + 4 - 2 * c) % NX
    col = lambda y_of: pl.ds(pl.multiple_of(c * HALF + y_of * WIDE, WIDE), WIDE)
    side = pl.ds(pl.multiple_of(c * HALF, HALF), HALF)
    pair_ks = pl.ds(2 * c, 2)

    barrier = pltpu.get_barrier_semaphore()
    partners = [device(z_to=(z + d) % NZ) for d in range(1, NZ)]
    partners += [device(x_to=(x + d) % NX) for d in range(1, NX)]
    partners += [device(y_to=(y + d) % NY) for d in range(1, NY)]
    partners += [sibling]
    for target in partners:
        pl.semaphore_signal(barrier, inc=1, device_id=target, device_id_type=MESH)
    for block in range(2):
        for half in range(2):
            own = jnp.logical_and(jnp.logical_and(2 * c + block == x, x == y), half == c)

            @pl.when(jnp.logical_not(own))
            def _():
                pl.semaphore_signal(
                    barrier, inc=1, device_id_type=MESH,
                    device_id=device(x_to=2 * c + block, y_to=x, c_to=half),
                )
    for y_of in range(NY):
        own = jnp.logical_and(jnp.logical_and(y == x, y_of == y), x // 2 == c)

        @pl.when(jnp.logical_not(own))
        def _():
            pl.semaphore_signal(
                barrier, inc=1, device_id_type=MESH,
                device_id=device(x_to=y, y_to=y_of, c_to=x // 2),
            )
    self_out = jnp.logical_and(x == y, x // 2 == c)

    low = pl.ds(pl.multiple_of(64 * (z % 2), 64), 64)
    for c_of in range(2):
        for y_of in range(NY):
            mats[z // 2, pair_ks, low, (c_of * NY + y_of) * WIDE : (c_of * NY + y_of + 1) * WIDE] = m_ref[
                :, :, (y_of * 2 + c_of) * WIDE : (y_of * 2 + c_of + 1) * WIDE
            ]
    own_copy = pltpu.make_async_copy(g_ref, grads.at[slot(x), 0:TOK, col(y)], l_sem.at[0])
    own_copy.start()

    rates_c = rates_col[0:96, :]
    state = jnp.zeros((96, WIDE), F32)
    for part in range(4):
        pos = lax.broadcasted_iota(jnp.int32, (96, 128), 1).astype(F32) + 128.0 * part
        dec_hi, dec_lo = split(jnp.exp(-pos * rates_c))
        rows = g_ref[128 * part : 128 * part + 128, :]
        state = state + mm(dec_hi, rows) + mm(dec_lo, rows)
    for group in range(12):
        for half in range(2):
            unit_out[group * 2 + half] = state[8 * group : 8 * group + 8, 128 * half : 128 * half + 128]
            unit_rates[group * 2 + half] = rates_col[8 * group : 8 * group + 8, :]

    pl.semaphore_wait(barrier, jnp.where(self_out, len(partners) + 6, len(partners) + 8))

    unit_copies = []
    for d in range(1, NZ):
        to = (z + d) % NZ
        copy = remote(
            unit_out.at[pl.ds(3 * to, 3)], unit_in.at[z], u_send.at[d], u_recv.at[d], device(z_to=to)
        )
        copy.start()
        unit_copies.append(copy)

    def piece(z_of, k):
        return mats.at[z_of // 2, 2 * c + k, pl.ds(pl.multiple_of(64 * (z_of % 2), 64), 64), :]

    m_wait, ms_wait = [], []

    def ring(d, k, way):
        z_of = (z + NZ - way * (d - 1)) % NZ
        ref = piece(z_of, k)
        i = ((d - 1) * 2 + k) * 2 + (way + 1) // 2
        copy = remote(ref, ref, m_send.at[i], m_recv.at[i], device(z_to=(z + NZ + way) % NZ))
        copy.start()
        m_wait.append(copy)
        return copy

    def arrive(copy, d, k, way):
        z_of = (z + NZ - way * d) % NZ
        ref = piece(z_of, k)
        i = ((d - 1) * 2 + k) * 2 + (way + 1) // 2
        copy.wait_recv()
        over = remote(ref, ref, ms_send.at[i], ms_recv.at[i], sibling)
        over.start()
        ms_wait.append(over)
        return over

    ring_copies = {}
    for k in range(2):
        for way in (1, -1):
            ring_copies[1, k, way] = ring(1, k, way)
    own_ref = mats.at[z // 2, pair_ks, low, :]
    own_over = remote(own_ref, own_ref, ms_send.at[16], ms_recv.at[16], sibling)
    own_over.start()

    over_copies = {}

    def event(d, k):
        for way in (1, -1):
            over_copies[d, k, way] = arrive(ring_copies[d, k, way], d, k, way)
            if d < 3 or (d == 3 and way == (1 if k == 0 else -1)):
                ring_copies[d + 1, k, way] = ring(d + 1, k, way)

    g_wait, gs_wait = [], []

    def send_g(base, i, src, dst, target):
        copy = remote(src, dst, g_send.at[base + i], g_recv.at[base + i], target)
        copy.start()
        g_wait.append(copy)
        return copy

    def over_g(base, i, src, dst):
        copy = remote(src, dst, gs_send.at[base + i], gs_recv.at[base + i], sibling)
        copy.start()
        gs_wait.append(copy)

    north = lambda d: (y + NY + d) % NY
    east = lambda d: (x + NX + d) % NX
    to_y = lambda d: device(y_to=north(d))
    to_x = lambda d: device(x_to=east(d))

    class YThenX:
        def __init__(self, n, row, size, cut):
            self.base, self.over = 8 * n, 4 * n
            self.rows = pl.ds(row, size)
            self.first, self.last = pl.ds(row, cut), pl.ds(row + cut, size - cut)

        def start(self, src):
            ref = grads.at[slot(x), self.rows, col(y)]
            src = ref if src is None else src
            self.a = send_g(self.base, 0, src, ref, to_y(1))
            self.b = send_g(self.base, 1, src, ref, to_y(-1))

        def relay(self):
            self.a.wait_recv()
            ref = grads.at[slot(x), self.first, col(north(-1))]
            self.d = send_g(self.base, 2, ref, ref, to_y(1))
            self.b.wait_recv()
            ref = grads.at[slot(x), self.last, col(north(1))]
            self.e = send_g(self.base, 3, ref, ref, to_y(-1))

        def turn(self):
            self.d.wait_recv()
            self.e.wait_recv()
            ref = grads.at[slot(x), self.rows, side]
            self.a = send_g(self.base, 4, ref, ref, to_x(1))
            self.b = send_g(self.base, 5, ref, ref, to_x(-1))

        def relay_again(self):
            self.a.wait_recv()
            ref = grads.at[slot(east(-1)), self.first, side]
            self.d = send_g(self.base, 6, ref, ref, to_x(1))
            self.b.wait_recv()
            ref = grads.at[slot(east(1)), self.last, side]
            self.e = send_g(self.base, 7, ref, ref, to_x(-1))
            mine = x // 2 == 1 - c
            opposite = east(2)
            buddy = lambda v: v + 1 - 2 * (v % 2)
            self.share(0, slot(jnp.where(mine, x, buddy(opposite))))
            self.second = slot(jnp.where(mine, buddy(x), opposite))

        def share(self, i, s):
            over_g(self.over, i, grads.at[s, self.rows, side], grads.at[s - 2, self.rows, side])

        def finish(self):
            self.d.wait_recv()
            self.e.wait_recv()
            self.share(1, self.second)

    class XThenY:
        def __init__(self, n, row, size, cut):
            self.base, self.over = 8 * n, 4 * n
            self.rows = pl.ds(row, size)
            self.first, self.last = pl.ds(row, cut), pl.ds(row + cut, size - cut)

        def start(self, src):
            ref = grads.at[slot(x), self.rows, col(y)]
            src = ref if src is None else src
            self.a = send_g(self.base, 0, src, ref, to_x(1))
            self.b = send_g(self.base, 1, src, ref, to_x(-1))

        def relay(self):
            self.a.wait_recv()
            ref = grads.at[slot(east(-1)), self.first, col(y)]
            self.d = send_g(self.base, 2, ref, ref, to_x(1))
            self.b.wait_recv()
            ref = grads.at[slot(east(1)), self.last, col(y)]
            self.e = send_g(self.base, 3, ref, ref, to_x(-1))

        def turn(self):
            self.d.wait_recv()
            self.e.wait_recv()
            ref = grads.at[:, self.rows, col(y)]
            self.a = send_g(self.base, 4, ref, ref, to_y(1))
            self.b = send_g(self.base, 5, ref, ref, to_y(-1))
            self.share(0, y)

        def relay_again(self):
            self.a.wait_recv()
            ref = grads.at[:, self.first, col(north(-1))]
            self.d = send_g(self.base, 6, ref, ref, to_y(1))
            self.b.wait_recv()
            ref = grads.at[:, self.last, col(north(1))]
            self.e = send_g(self.base, 7, ref, ref, to_y(-1))
            self.share(1, north(-1))
            self.share(2, north(1))

        def share(self, i, y_of):
            over_g(
                self.over, i, grads.at[2:4, self.rows, col(y_of)], grads.at[0:2, self.rows, col(y_of)]
            )

        def finish(self):
            self.d.wait_recv()
            self.e.wait_recv()
            self.share(3, north(2))

    tok_a, tok_b = YThenX(0, 0, 256, 128), XThenY(1, 256, 256, 128)
    ent_a, ent_b = YThenX(2, HI, POLES, 48), XThenY(3, LO, POLES, 48)

    tok_a.start(g_ref.at[0:256, :])
    tok_b.start(g_ref.at[256:512, :])

    own_units = pl.ds(3 * z, 3)
    lam = jnp.exp(-float(TOK) * unit_rates[own_units])
    unit_in[z] = unit_out[own_units]
    for copy in unit_copies:
        copy.wait_recv()
    run = jnp.zeros((3, 8, 128), F32)
    for z_of in range(NZ - 1, -1, -1):
        enter_out[z_of] = run
        run = unit_in[z_of] + lam * run
    total_out[...] = run
    total_in[x] = run
    total_copies = []
    for d in range(1, NX):
        copy = remote(
            total_out, total_in.at[x], t_send.at[d], t_recv.at[d], device(x_to=(x + d) % NX)
        )
        copy.start()
        total_copies.append(copy)

    tok_a.relay()
    tok_b.relay()

    rates_r = rates_row[0:1, :]
    rise_pos = lax.broadcasted_iota(jnp.int32, (TOK, 128), 0).astype(F32)
    falling = jnp.exp((rise_pos - 256.0) * rates_r)
    rising = jnp.exp((256.0 - rise_pos) * rates_r)
    edge = gains_row[0:1, :] * jnp.exp((rise_pos - float(TOK)) * rates_r)
    edge_hi[...], edge_lo[...] = split(edge)

    def taps(th, k):
        size = 256 * (th + 1)
        scaled = rising[256 * th : 256 * th + 256] * (coef_row[y, k : k + 1, :] * gains_row[0:1, :])
        mat = lax.dot_general(
            falling[0:size], scaled, NT, precision=lax.Precision.HIGHEST, preferred_element_type=F32
        )
        s_at = lax.broadcasted_iota(jnp.int32, (size, 256), 0)
        t_at = lax.broadcasted_iota(jnp.int32, (size, 256), 1) + 256 * th
        high, rest = split(jnp.where(t_at >= s_at, mat, 0.0))
        at = th * HALF + k * 256
        kern_hi[0:size, at : at + 256] = high
        kern_lo[0:size, at : at + 256] = rest

    for k in range(4):
        taps(0, k)
    own_copy.wait()
    tok_a.turn()
    tok_b.turn()
    event(1, 0)

    for copy in total_copies:
        copy.wait_recv()
    lam_row = jnp.exp(-float(TOK * NZ) * unit_rates[own_units])
    carry = jnp.zeros((3, 8, 128), F32)
    for x_of in range(NX - 1, 0, -1):
        carry = jnp.where(x_of > x, total_in[x_of] + lam_row * carry, carry)
    for z_of in range(NZ - 1, -1, -1):
        enter_out[z_of] = enter_out[z_of] + carry
        carry = lam * carry
    enter_copies = []
    for d in range(1, NZ):
        to = (z + d) % NZ
        copy = remote(
            enter_out.at[to], enter_in.at[own_units], e_send.at[d], e_recv.at[d], device(z_to=to)
        )
        copy.start()
        enter_copies.append(copy)
    enter_in[own_units] = enter_out[z]

    for k in range(4):
        taps(1, k)
        coef_col[k] = jnp.broadcast_to(coef_row[y, k : k + 1, :], (128, 128)).T
    state_hi[...] = jnp.zeros_like(state_hi)
    state_lo[...] = jnp.zeros_like(state_lo)
    event(1, 1)
    for d in range(1, NZ):
        source = (z + NZ - d) % NZ
        remote(
            enter_out.at[0], enter_in.at[pl.ds(3 * source, 3)], e_send.at[d], e_recv.at[d], sibling
        ).wait_recv()
    for group in range(10):
        for half in range(2):
            high, rest = split(enter_in[group * 2 + half])
            grads_cols = pl.ds(pl.multiple_of(c * HALF + y * WIDE + 128 * half, 128), 128)
            grads[slot(x), HI + 8 * group : HI + 8 * group + 8, grads_cols] = high
            grads[slot(x), LO + 8 * group : LO + 8 * group + 8, grads_cols] = rest
    ent_a.start(None)
    ent_b.start(None)
    tok_a.relay_again()
    tok_b.relay_again()
    event(2, 0)
    ent_a.relay()
    ent_b.relay()
    tok_a.finish()
    tok_b.finish()
    ent_a.turn()
    ent_b.turn()
    event(2, 1)

    def near(q):
        filters = mats.at[q]

        @pl.loop(0, 4)
        def _(step):
            block, th = step // 2, step % 2
            rows = grads[block, pl.ds(pl.multiple_of(th * 256, 256), 256), :]
            for k in range(4):
                high, rest = split(mm(rows, filters[k], NT))
                at = pl.ds(pl.multiple_of(th * HALF + k * 256, 256), 256)
                lanes = pl.ds(pl.multiple_of(block * 128, 128), 128)
                proj_hi[at, lanes] = high
                proj_lo[at, lanes] = rest

        for sh in range(2):
            s_rows, t_rows = slice(256 * sh, 256 * sh + 256), slice(HALF * sh, D)
            acc = (
                mm(kern_hi[s_rows, t_rows], proj_hi[t_rows, :])
                + mm(kern_hi[s_rows, t_rows], proj_lo[t_rows, :])
                + mm(kern_lo[s_rows, t_rows], proj_hi[t_rows, :])
            )
            parts[q, 0, s_rows, :] = acc[:, 0:128]
            parts[q, 1, s_rows, :] = acc[:, 128:256]

    out_waits = []

    def far(n, q):
        for block in range(2):
            total = jnp.zeros((POLES, 128), F32)
            for k in range(4):
                both = mm(grads[block, HI:ROWS, :], mats[q, k], NT)
                total = total + coef_col[k, 0:POLES, :] * (both[0:POLES] + both[POLES : 2 * POLES])
            high, rest = split(total)
            state_hi[0:POLES, 128 * block : 128 * block + 128] = high
            state_lo[0:POLES, 128 * block : 128 * block + 128] = rest
        acc = (
            mm(edge_hi[...], state_hi[...])
            + mm(edge_hi[...], state_lo[...])
            + mm(edge_lo[...], state_hi[...])
        )
        for block in range(2):
            parts[q, block] = parts[q, block] + acc[:, 128 * block : 128 * block + 128]
            own = jnp.logical_and(jnp.logical_and(2 * c + block == x, x == y), q // 2 == c)
            cols = pl.ds(pl.multiple_of((q % 2) * 128, 128), 128)
            i = 2 * n + block
            away = remote(
                parts.at[q, block], arrived.at[y, :, cols], o_send.at[i], o_recv.at[y, q % 2],
                device(x_to=2 * c + block, y_to=x, c_to=q // 2),
            )
            local = pltpu.make_async_copy(
                parts.at[q, block], arrived.at[y, :, cols], o_recv.at[y, q % 2]
            )

            @pl.when(jnp.logical_not(own))
            def _():
                away.start()

            @pl.when(own)
            def _():
                local.start()

            out_waits.append((own, away))

    def over_in(d, k):
        for way in (1, -1):
            if (d, k, way) in over_copies:
                over_copies[d, k, way].wait_recv()

    def last_event():
        for k, way in ((0, 1), (1, -1)):
            over_copies[4, k, way] = arrive(ring_copies[4, k, way], 4, k, way)

    q_own = z // 2
    lean = 1 - 2 * (z % 2)
    order = [q_own, (q_own + 4 - lean) % 4, (q_own + 4 + lean) % 4, (q_own + 2) % 4]

    def g_over_in(lo, hi):
        for copy in gs_wait[lo:hi]:
            copy.wait_recv()

    own_over.wait_recv()
    over_in(1, 0)
    over_in(1, 1)
    shared = len(gs_wait)
    g_over_in(0, shared)
    near(order[0])
    event(3, 0)
    ent_a.relay_again()
    ent_b.relay_again()
    over_in(2, 0)
    over_in(2, 1)
    near(order[1])
    ent_a.finish()
    ent_b.finish()
    event(3, 1)
    g_over_in(shared, len(gs_wait))
    far(0, order[0])
    far(1, order[1])
    over_in(3, 0)
    over_in(3, 1)
    near(order[2])
    far(2, order[2])
    last_event()
    over_in(4, 0)
    over_in(4, 1)
    near(order[3])
    far(3, order[3])

    for y_of in range(NY):
        for half in range(2):
            ref = arrived.at[y_of, :, 128 * half : 128 * half + 128]
            pltpu.make_async_copy(ref, ref, o_recv.at[y_of, half]).wait()
    out_ref[...] = (arrived[0] + arrived[1] + arrived[2] + arrived[3]).astype(BF16)

    for copy in unit_copies + total_copies + enter_copies + m_wait + ms_wait + g_wait + gs_wait + [own_over]:
        copy.wait_send()
    for own, away in out_waits:

        @pl.when(jnp.logical_not(own))
        def _():
            away.wait_send()


def per_device(out_grad, filter_mats, coeffs, pole_rates):
    rates = jnp.pad(pole_rates, (0, 128 - POLES))
    gains = jnp.sqrt(-jnp.expm1(-2.0 * rates))
    rates_col = jnp.broadcast_to(rates[:, None], (128, 128))
    rates_row = jnp.broadcast_to(rates[None, :], (8, 128))
    gains_row = jnp.broadcast_to(gains[None, :], (8, 128))
    coef_row = jnp.pad(coeffs, ((0, 0), (0, 128 - POLES))).reshape(4, 4, 128)
    dma = pltpu.SemaphoreType.DMA
    vmem = pl.BlockSpec(memory_space=pltpu.VMEM)
    return pl.pallas_call(
        kernel,
        out_shape=jax.ShapeDtypeStruct((TOK, WIDE), BF16),
        in_specs=[vmem] * 6,
        out_specs=vmem,
        scratch_shapes=[
            pltpu.VMEM((NX, ROWS, D), BF16),
            pltpu.VMEM((4, 4, 128, D), BF16),
            pltpu.VMEM((TOK, D), BF16),
            pltpu.VMEM((TOK, D), BF16),
            pltpu.VMEM((D, 256), BF16),
            pltpu.VMEM((D, 256), BF16),
            pltpu.VMEM((4, 2, TOK, 128), F32),
            pltpu.VMEM((NY, TOK, WIDE), F32),
            pltpu.VMEM((TOK, 128), BF16),
            pltpu.VMEM((TOK, 128), BF16),
            pltpu.VMEM((128, 256), BF16),
            pltpu.VMEM((128, 256), BF16),
            pltpu.VMEM((4, 128, 128), F32),
            pltpu.VMEM((UNITS, 8, 128), F32),
            pltpu.VMEM((UNITS, 8, 128), F32),
            pltpu.VMEM((NZ, 3, 8, 128), F32),
            pltpu.VMEM((3, 8, 128), F32),
            pltpu.VMEM((NX, 3, 8, 128), F32),
            pltpu.VMEM((NZ, 3, 8, 128), F32),
            pltpu.VMEM((UNITS, 8, 128), F32),
            dma((32,)), dma((32,)), dma((16,)), dma((16,)),
            dma((16,)), dma((16,)), dma((17,)), dma((17,)),
            dma((NZ,)), dma((NZ,)), dma((NX,)), dma((NX,)), dma((NZ,)), dma((NZ,)),
            dma((8,)), dma((NY, 2)), dma((1,)),
        ],
        compiler_params=pltpu.CompilerParams(
            collective_id=0, has_side_effects=True, vmem_limit_bytes=60 * 1024 * 1024
        ),
        name="spectral_grad",
    )(out_grad, filter_mats, rates_col, rates_row, gains_row, coef_row)


def solution(mesh):
    placed = (P("ctx", "grp"), P("grp", "ctx", None), P(), P())
    return jax.shard_map(
        per_device, mesh=mesh, in_specs=placed, out_specs=P("ctx", "grp"), check_vma=False
    )
```

```python
import jax
import jax.numpy as jnp
from jax import lax
from jax.experimental import pallas as pl
from jax.experimental.pallas import tpu as pltpu
from jax.sharding import PartitionSpec as P

MESH = pl.DeviceIdType.MESH
F32, BF16 = jnp.float32, jnp.bfloat16
NX, NZ, NY = 4, 8, 4
TOK, WIDE, HALF, D = 512, 256, 1024, 2048
POLES, UNITS = 80, 24
HI = TOK
LO = TOK + POLES
ROWS = TOK + 2 * POLES
NT = (((1,), (1,)), ((), ()))
NN = (((1,), (0,)), ((), ()))
OFFSETS = (0, -1, 1, 2)


def split(value):
    high = value.astype(BF16)
    return high, (value - high.astype(F32)).astype(BF16)


def mm(a, b, dims=NN):
    return lax.dot_general(a, b, dims, preferred_element_type=F32)


def minus_expm1_neg(u):
    series = jnp.ones_like(u)
    for n in range(9, 1, -1):
        series = 1.0 - u * (1.0 / n) * series
    return jnp.where(u < 0.25, u * series, 1.0 - jnp.exp(-u))


def kernel(
    g_ref, m_ref, rates_ref, coeffs_ref, out_ref,
    grads, mats, kern_hi, kern_lo, proj_hi, proj_lo, parts, arrived, edge_hi, edge_lo,
    state_hi, state_lo, coef_col, rates_row, coef_row, rates_col, unit_rates, unit_out, unit_in,
    total_out, total_in, enter_out, enter_in,
    p1_send, p1_recv, p2_send, p2_recv, rl_send, rl_recv, sh_send, sh_recv,
    g_send, g_recv, m_send, m_recv, ms_send, ms_recv, u_send, u_recv,
    t_send, t_recv, e_send, e_recv, o_send, o_recv, l_sem,
):
    ctx, grp = lax.axis_index("ctx"), lax.axis_index("grp")
    x, z, y, c = ctx // NZ, ctx % NZ, grp // 2, grp % 2

    def device(x_to=None, z_to=None, y_to=None, c_to=None):
        pick = lambda new, own: own if new is None else new
        return (pick(x_to, x) * NZ + pick(z_to, z), pick(y_to, y) * 2 + pick(c_to, c))

    def remote(src, dst, send, recv, target):
        copy = pltpu.make_async_remote_copy(
            src_ref=src, dst_ref=dst, send_sem=send, recv_sem=recv,
            device_id=target, device_id_type=MESH,
        )
        return copy

    sibling = device(c_to=1 - c)
    slot = lambda x_of: (x_of + 4 - 2 * c) % NX
    col = lambda y_of: pl.ds(pl.multiple_of(c * HALF + y_of * WIDE, WIDE), WIDE)
    side = pl.ds(pl.multiple_of(c * HALF, HALF), HALF)

    barrier = pltpu.get_barrier_semaphore()
    partners = [device(z_to=(z + d) % NZ) for d in range(1, NZ)]
    partners += [device(x_to=(x + d) % NX) for d in range(1, NX)]
    partners += [device(y_to=(y + d) % NY) for d in range(1, NY)]
    partners += [sibling]
    for target in partners:
        pl.semaphore_signal(barrier, inc=1, device_id=target, device_id_type=MESH)
    for block in range(2):
        for half in range(2):
            own = jnp.logical_and(jnp.logical_and(2 * c + block == x, x == y), half == c)

            @pl.when(jnp.logical_not(own))
            def _():
                pl.semaphore_signal(
                    barrier, inc=1, device_id_type=MESH,
                    device_id=device(x_to=2 * c + block, y_to=x, c_to=half),
                )
    for y_of in range(NY):
        own = jnp.logical_and(jnp.logical_and(y == x, y_of == y), x // 2 == c)

        @pl.when(jnp.logical_not(own))
        def _():
            pl.semaphore_signal(
                barrier, inc=1, device_id_type=MESH,
                device_id=device(x_to=y, y_to=y_of, c_to=x // 2),
            )
    self_out = jnp.logical_and(x == y, x // 2 == c)

    low = pl.ds(pl.multiple_of(64 * (z % 2), 64), 64)
    for c_of in range(2):
        for y_of in range(NY):
            mats[z // 2, :, c, low, (c_of * NY + y_of) * WIDE : (c_of * NY + y_of + 1) * WIDE] = m_ref[
                :, :, (y_of * 2 + c_of) * WIDE : (y_of * 2 + c_of + 1) * WIDE
            ]
    own_copy = pltpu.make_async_copy(g_ref, grads.at[slot(x), 0:TOK, col(y)], l_sem.at[0])
    own_copy.start()

    rates_row[...] = jnp.zeros_like(rates_row)
    coef_row[...] = jnp.zeros_like(coef_row)
    rates_row[0:1, 0:POLES] = rates_ref[...]
    coef_row[:, 0:POLES] = coeffs_ref[...]
    rates_col[...] = jnp.broadcast_to(rates_row[0:1, :], (128, 128)).T
    gains = jnp.sqrt(minus_expm1_neg(2.0 * rates_row[0:1, :]))
    rates_c = rates_col[0:POLES, :]
    state = jnp.zeros((POLES, WIDE), F32)
    for part in range(4):
        pos = lax.broadcasted_iota(jnp.int32, (POLES, 128), 1).astype(F32) + 128.0 * part
        dec_hi, dec_lo = split(jnp.exp(-pos * rates_c))
        rows = g_ref[128 * part : 128 * part + 128, :]
        state = state + mm(dec_hi, rows) + mm(dec_lo, rows)
    for group in range(10):
        for half in range(2):
            unit_out[group * 2 + half] = state[8 * group : 8 * group + 8, 128 * half : 128 * half + 128]
            unit_rates[group * 2 + half] = rates_col[8 * group : 8 * group + 8, :]

    pl.semaphore_wait(barrier, jnp.where(self_out, len(partners) + 6, len(partners) + 8))

    unit_copies = []
    for d in range(1, NZ):
        to = (z + d) % NZ
        copy = remote(
            unit_out.at[pl.ds(3 * to, 3)], unit_in.at[z], u_send.at[d], u_recv.at[d], device(z_to=to)
        )
        copy.start()
        unit_copies.append(copy)

    g_wait, sent = [], []

    def send_g(i, j, src, dst, target):
        copy = remote(src, dst, g_send.at[i], g_recv.at[j], target)
        copy.start()
        g_wait.append(copy)

    north = lambda d: (y + NY + d) % NY
    east = lambda d: (x + NX + d) % NX
    to_y = lambda d: device(y_to=north(d))
    to_x = lambda d: device(x_to=east(d))

    hi_rows, lo_rows = pl.ds(HI, POLES), pl.ds(LO, POLES)

    def states_first():
        for d in range(1, 4):
            ref = grads.at[slot(x), hi_rows, col(y)]
            send_g(d - 1, d - 1, ref, ref, to_y(d))
            ref = grads.at[slot(x), lo_rows, col(y)]
            send_g(3 + d - 1, 3 + d - 1, ref, ref, to_x(d))

    def states_second():
        for copy in g_wait[0:6]:
            copy.wait_recv()
        ref, dst = grads.at[slot(x), hi_rows, side], grads.at[x % 2, hi_rows, side]
        for d in range(1, 4):
            send_g(6 + d - 1, 6 + 2 * (x % 2) + c, ref, dst, device(x_to=east(d), c_to=x // 2))
        hi_over = remote(ref, dst, g_send.at[9], g_recv.at[6 + 2 * (x % 2) + c], sibling)

        @pl.when(x // 2 != c)
        def _():
            hi_over.start()

        dst = grads.at[0:2, lo_rows, col(y)]
        away = grads.at[2:4, lo_rows, col(y)]
        for d in range(1, 4):
            send_g(9 + d, 10 + 2 * y + c, dst, dst, to_y(d))
            send_g(12 + d, 10 + 2 * y + c, away, dst, device(y_to=north(d), c_to=1 - c))
        send_g(16, 10 + 2 * y + c, away, dst, sibling)
        return hi_over

    def states_finish():
        ref = grads.at[0, hi_rows, side]
        for b in range(2):
            for c_of in range(2):

                @pl.when(jnp.logical_not(jnp.logical_and(2 * c + b == x, c_of == c)))
                def _():
                    remote(ref, ref, g_send.at[0], g_recv.at[6 + 2 * b + c_of], sibling).wait_recv()

        ref2 = grads.at[0:2, lo_rows, col(y)]
        for y_of in range(NY):
            for c_of in range(2):

                @pl.when(jnp.logical_not(jnp.logical_and(y_of == y, c_of == c)))
                def _():
                    remote(ref2, ref2, g_send.at[0], g_recv.at[10 + 2 * y_of + c_of], sibling).wait_recv()

    class Tokens:
        def __init__(self, n, row, y_first):
            self.n, self.y_first = n, y_first
            self.rows, self.first, self.last = pl.ds(row, 256), pl.ds(row, 128), pl.ds(row + 128, 128)
            self.src = g_ref.at[row : row + 256, :]
            self.hop1, self.hop2 = (to_y, to_x) if y_first else (to_x, to_y)
            self.p1, self.p2, self.shares = {}, {}, []

        def ref(self, d1, d2, rows, s=None):
            dx, dy = (d2, d1) if self.y_first else (d1, d2)
            return grads.at[slot(east(dx)) if s is None else s, rows, col(north(dy))]

        def copy(self, src, dst, i, target, first=True):
            send, recv = (p1_send, p1_recv) if first else (p2_send, p2_recv)
            copy = remote(src, dst, send.at[self.n, i], recv.at[self.n, i], target)
            copy.start()
            sent.append(copy)
            return copy

        def onward(self, j, src=None):
            ref = self.ref(OFFSETS[j], 0, self.rows)
            for way in (1, -1):
                self.p2[j, way] = self.copy(
                    ref if src is None else src, ref, 2 * j + (way + 1) // 2, self.hop2(way), False
                )

        def start(self):
            ref = self.ref(0, 0, self.rows)
            self.p1[0] = self.copy(self.src, ref, 0, self.hop1(1))
            self.p1[1] = self.copy(self.src, ref, 1, self.hop1(-1))

        def mid(self):
            for i, way, rows in ((0, 1, self.first), (1, -1, self.last)):
                self.p1[i].wait_recv()
                ref = self.ref(-way, 0, rows)
                self.p1[i + 2] = self.copy(ref, ref, i + 2, self.hop1(way))

        def opposite(self):
            self.p1[2].wait_recv()
            self.p1[3].wait_recv()
            self.onward(3)

        def relay(self, j):
            for way, rows in ((1, self.first), (-1, self.last)):
                self.p2[j, way].wait_recv()
                owner = east(-way) if self.y_first else east(OFFSETS[j])
                at = 8 * c + 2 * j + (way + 1) // 2 if self.y_first else 4 * c + 2 * (owner % 2) + (way + 1) // 2
                target = (
                    device(x_to=east(way), c_to=owner // 2)
                    if self.y_first
                    else device(y_to=north(way), c_to=owner // 2)
                )
                copy = remote(
                    self.ref(OFFSETS[j], -way, rows), self.ref(OFFSETS[j], -way, rows, owner % 2),
                    rl_send.at[self.n, 2 * j + (way + 1) // 2], rl_recv.at[self.n, at], target,
                )
                copy.start()
                sent.append(copy)

        def share_copy(self, i, src, dst):
            return remote(src, dst, sh_send.at[self.n, i], sh_recv.at[self.n, i], sibling)

        def share(self):
            if self.y_first:
                mine = x // 2 == 1 - c
                buddy = lambda v: v + 1 - 2 * (v % 2)
                s0 = slot(jnp.where(mine, x, buddy(east(2))))
                s1 = slot(jnp.where(mine, buddy(x), x))
                at = lambda s: grads.at[s, self.rows, side]
                copy = self.share_copy(0, at(s0), at(s0 - 2))
                copy.start()
                sent.append(copy)
                self.shares.append(copy)
                self.extra = self.share_copy(1, at(jnp.where(mine, s1, 2)), at(jnp.where(mine, s1 - 2, 0)))

                @pl.when(mine)
                def _():
                    self.extra.start()
            else:
                for i, dy in enumerate((0, -1, 1)):
                    at = lambda lo: grads.at[lo : lo + 2, self.rows, col(north(dy))]
                    copy = self.share_copy(i, at(2), at(0))
                    copy.start()
                    sent.append(copy)
                    self.shares.append(copy)

        def finish(self):
            for copy in self.shares:
                copy.wait_recv()
            piece_ref = grads.at[0, self.first, 0:WIDE]

            def wait_relays(count):
                for at in range(count):
                    remote(
                        piece_ref, piece_ref, rl_send.at[self.n, 0], rl_recv.at[self.n, at], sibling
                    ).wait_recv()

            if self.y_first:

                @pl.when(x // 2 == c)
                def _():
                    self.extra.wait_recv()

                @pl.when(east(2) // 2 == c)
                def _():
                    wait_relays(16)
            else:
                wait_relays(8)

        def drain(self):
            if self.y_first:

                @pl.when(x // 2 == 1 - c)
                def _():
                    self.extra.wait_send()

    tok_a, tok_b = Tokens(0, 0, True), Tokens(1, 256, False)

    tok_a.start()
    tok_b.start()
    tok_a.onward(0, tok_a.src)
    tok_b.onward(0, tok_b.src)

    def piece(z_of, d, k, way):
        start, size = 64 * (z_of % 2), 64
        if d == 4:
            start, size = start + 16 * (1 - way), 32
        return mats.at[z_of // 2, k, c, pl.ds(pl.multiple_of(start, 32), size), :]

    m_wait, ms_wait = [], []

    def ring(d, k, way):
        z_of = (z + NZ - way * (d - 1)) % NZ
        ref = piece(z_of, d, k, way)
        i = ((d - 1) * 2 + k) * 2 + (way + 1) // 2
        copy = remote(ref, ref, m_send.at[i], m_recv.at[i], device(z_to=(z + NZ + way) % NZ))
        copy.start()
        m_wait.append(copy)
        return copy

    def arrive(copy, d, k, way):
        z_of = (z + NZ - way * d) % NZ
        ref = piece(z_of, d, k, way)
        i = ((d - 1) * 2 + k) * 2 + (way + 1) // 2
        copy.wait_recv()
        over = remote(ref, ref, ms_send.at[i], ms_recv.at[i], sibling)
        over.start()
        ms_wait.append(over)
        return over

    ring_copies = {}
    for k in range(2):
        for way in (1, -1):
            ring_copies[1, k, way] = ring(1, k, way)
    own_ref = mats.at[z // 2, :, c, low, :]
    own_over = remote(own_ref, own_ref, ms_send.at[16], ms_recv.at[16], sibling)
    own_over.start()

    over_copies = {}

    def event(d, k):
        for way in (1, -1):
            over_copies[d, k, way] = arrive(ring_copies[d, k, way], d, k, way)
            if d < 4:
                ring_copies[d + 1, k, way] = ring(d + 1, k, way)

    own_units = pl.ds(3 * z, 3)
    total_copies, enter_copies = [], []

    def hand_on():
        lam = jnp.exp(-float(TOK) * unit_rates[own_units])
        unit_in[z] = unit_out[own_units]
        for copy in unit_copies:
            copy.wait_recv()
        run = jnp.zeros((3, 8, 128), F32)
        for z_of in range(NZ - 1, -1, -1):
            enter_out[z_of] = run
            run = unit_in[z_of] + lam * run
        total_out[...] = run
        total_in[x] = run
        for d in range(1, NX):
            copy = remote(
                total_out, total_in.at[x], t_send.at[d], t_recv.at[d], device(x_to=(x + d) % NX)
            )
            copy.start()
            total_copies.append(copy)

    def send_enter():
        for copy in total_copies:
            copy.wait_recv()
        lam_row = jnp.exp(-float(TOK * NZ) * unit_rates[own_units])
        carry = jnp.zeros((3, 8, 128), F32)
        for x_of in range(NX - 1, 0, -1):
            carry = jnp.where(x_of > x, total_in[x_of] + lam_row * carry, carry)
        lam = jnp.exp(-float(TOK) * unit_rates[own_units])
        for z_of in range(NZ - 1, -1, -1):
            enter_out[z_of] = enter_out[z_of] + carry
            carry = lam * carry
        for d in range(1, NZ):
            to = (z + d) % NZ
            copy = remote(
                enter_out.at[to], enter_in.at[own_units], e_send.at[d], e_recv.at[d], device(z_to=to)
            )
            copy.start()
            enter_copies.append(copy)
        enter_in[own_units] = enter_out[z]

    def store_enter():
        for d in range(1, NZ):
            source = (z + NZ - d) % NZ
            remote(
                enter_out.at[0], enter_in.at[pl.ds(3 * source, 3)], e_send.at[d], e_recv.at[d], sibling
            ).wait_recv()
        for group in range(10):
            for half in range(2):
                high, rest = split(enter_in[group * 2 + half])
                grads_cols = pl.ds(pl.multiple_of(c * HALF + y * WIDE + 128 * half, 128), 128)
                grads[slot(x), HI + 8 * group : HI + 8 * group + 8, grads_cols] = high
                grads[slot(x), LO + 8 * group : LO + 8 * group + 8, grads_cols] = rest

    rates_r = rates_row[0:1, :]
    rise_pos = lax.broadcasted_iota(jnp.int32, (TOK, 128), 0).astype(F32)
    falling = jnp.exp((rise_pos - 256.0) * rates_r)
    rising = jnp.exp((256.0 - rise_pos) * rates_r)
    edge = gains * jnp.exp((rise_pos - float(TOK)) * rates_r)
    edge_hi[...], edge_lo[...] = split(edge)

    def taps(th, k):
        size = 256 * (th + 1)
        scaled = rising[256 * th : 256 * th + 256] * (coef_row[pl.ds(4 * y + k, 1), :] * gains)
        mat = lax.dot_general(
            falling[0:size], scaled, NT, precision=lax.Precision.HIGHEST, preferred_element_type=F32
        )
        s_at = lax.broadcasted_iota(jnp.int32, (size, 256), 0)
        t_at = lax.broadcasted_iota(jnp.int32, (size, 256), 1) + 256 * th
        high, rest = split(jnp.where(t_at >= s_at, mat, 0.0))
        at = (k % 2) * HALF + th * TOK + (k // 2) * 256
        kern_hi[0:size, at : at + 256] = high
        kern_lo[0:size, at : at + 256] = rest

    def more_taps(ks):
        for k in ks:
            taps(1, k)
            coef_col[k] = jnp.broadcast_to(coef_row[pl.ds(4 * y + k, 1), :], (128, 128)).T

    tok_a.mid()
    tok_b.mid()
    hand_on()
    for j in (1, 2):
        tok_a.onward(j)
        tok_b.onward(j)
    for k in range(4):
        taps(0, k)
    own_copy.wait()
    tok_a.opposite()
    tok_b.opposite()
    send_enter()
    event(1, 0)
    tok_a.relay(0)
    tok_b.relay(0)
    more_taps((0, 1))
    tok_a.relay(1)
    tok_b.relay(1)
    event(1, 1)
    tok_a.relay(2)
    tok_b.relay(2)
    state_hi[...] = jnp.zeros_like(state_hi)
    state_lo[...] = jnp.zeros_like(state_lo)
    store_enter()
    states_first()
    tok_a.relay(3)
    tok_b.relay(3)
    tok_a.share()
    tok_b.share()
    more_taps((2,))
    event(2, 0)
    more_taps((3,))

    def project(q, kk):
        weights = mats[q, kk].reshape(256, D)
        parts_of = [(block, th) for block in range(2) for th in range(2)]
        tiles = [mm(grads[block, 256 * th : 256 * th + 256, :], weights, NT) for block, th in parts_of]
        for (block, th), tile in zip(parts_of, tiles):
            high, rest = split(tile)
            for c_of in range(2):
                at = kk * HALF + th * TOK + c_of * 256
                lanes, own = slice(128 * block, 128 * block + 128), slice(128 * c_of, 128 * c_of + 128)
                proj_hi[at : at + 256, lanes] = high[:, own]
                proj_lo[at : at + 256, lanes] = rest[:, own]

    def near(sh, kk):
        s_rows = slice(256 * sh, 256 * sh + 256)
        t_rows = slice(HALF * kk + TOK * sh, HALF * kk + HALF)
        return (
            mm(kern_hi[s_rows, t_rows], proj_hi[t_rows, :])
            + mm(kern_hi[s_rows, t_rows], proj_lo[t_rows, :])
            + mm(kern_lo[s_rows, t_rows], proj_hi[t_rows, :])
        )

    def enter(q):
        both = mm(grads[0:2, HI:ROWS, :].reshape(4 * POLES, D), mats[q].reshape(512, D), NT)
        for block in range(2):
            total = jnp.zeros((POLES, 128), F32)
            top = 2 * POLES * block
            for kk in range(2):
                for c_of in range(2):
                    at = 256 * kk + 128 * c_of
                    lanes = slice(at, at + 128)
                    total = total + coef_col[2 * c_of + kk, 0:POLES, :] * (
                        both[top : top + POLES, lanes] + both[top + POLES : top + 2 * POLES, lanes]
                    )
            high, rest = split(total)
            state_hi[0:POLES, 128 * block : 128 * block + 128] = high
            state_lo[0:POLES, 128 * block : 128 * block + 128] = rest

    def far(sh):
        s_rows = slice(256 * sh, 256 * sh + 256)
        return (
            mm(edge_hi[s_rows, :], state_hi[...])
            + mm(edge_hi[s_rows, :], state_lo[...])
            + mm(edge_lo[s_rows, :], state_hi[...])
        )

    out_waits = []

    def deliver(n, q, sh):
        s_rows = slice(256 * sh, 256 * sh + 256)
        for block in range(2):
            own = jnp.logical_and(jnp.logical_and(2 * c + block == x, x == y), q // 2 == c)
            cols = pl.ds(pl.multiple_of((q % 2) * 128, 128), 128)
            src, dst = parts.at[n, block, s_rows, :], arrived.at[y, s_rows, cols]
            done = o_recv.at[y, 2 * (q % 2) + sh]
            away = remote(
                src, dst, o_send.at[4 * n + 2 * block + sh], done,
                device(x_to=2 * c + block, y_to=x, c_to=q // 2),
            )
            local = pltpu.make_async_copy(src, dst, done)

            @pl.when(jnp.logical_not(own))
            def _():
                away.start()

            @pl.when(own)
            def _():
                local.start()

            out_waits.append((own, away))

    def store(n, sh, value, add=False):
        s_rows = slice(256 * sh, 256 * sh + 256)
        for block in range(2):
            new = value[:, 128 * block : 128 * block + 128]
            parts[n, block, s_rows, :] = parts[n, block, s_rows, :] + new if add else new

    def over_in(d, k):
        for way in (1, -1):
            if (d, k, way) in over_copies:
                over_copies[d, k, way].wait_recv()

    q_own = z // 2
    lean = 1 - 2 * (z % 2)
    order = [q_own, (q_own + 4 - lean) % 4, (q_own + 4 + lean) % 4, (q_own + 2) % 4]

    own_over.wait_recv()
    over_in(1, 0)
    over_in(1, 1)
    tok_a.finish()
    tok_b.finish()
    project(order[0], 0)
    project(order[0], 1)
    event(2, 1)
    for sh in range(2):
        store(0, sh, near(sh, 0) + near(sh, 1))
    hi_over = states_second()
    over_in(2, 0)
    over_in(2, 1)
    project(order[1], 0)
    project(order[1], 1)
    event(3, 0)
    for sh in range(2):
        store(1, sh, near(sh, 0) + near(sh, 1))
    states_finish()
    for n in range(2):
        enter(order[n])
        for sh in range(2):
            store(n, sh, far(sh), True)
            deliver(n, order[n], sh)
    over_in(3, 0)
    project(order[2], 0)
    event(3, 1)
    for sh in range(2):
        store(2, sh, near(sh, 0))
    over_in(3, 1)
    project(order[2], 1)
    event(4, 0)
    enter(order[2])
    for sh in (1, 0):
        store(2, sh, near(sh, 1) + far(sh), True)
        deliver(2, order[2], sh)
    over_in(4, 0)
    project(order[3], 0)
    event(4, 1)
    for sh in range(2):
        store(3, sh, near(sh, 0))
    over_in(4, 1)
    project(order[3], 1)
    enter(order[3])
    for sh in (1, 0):
        store(3, sh, near(sh, 1) + far(sh), True)
        deliver(3, order[3], sh)

    for n in range(4):
        q = order[n]

        @pl.when(q // 2 == c)
        def _():
            cols = pl.ds(pl.multiple_of((q % 2) * 128, 128), 128)
            for sh in (1, 0):
                s_rows = slice(256 * sh, 256 * sh + 256)
                for y_of in range(NY):
                    ref = arrived.at[y_of, s_rows, cols]
                    pltpu.make_async_copy(ref, ref, o_recv.at[y_of, 2 * (q % 2) + sh]).wait()
                total = arrived[0, s_rows, cols] + arrived[1, s_rows, cols]
                total = total + arrived[2, s_rows, cols] + arrived[3, s_rows, cols]
                out_ref[s_rows, cols] = total.astype(BF16)

    tok_a.drain()

    @pl.when(x // 2 != c)
    def _():
        hi_over.wait_send()

    for copy in unit_copies + total_copies + enter_copies + m_wait + ms_wait + g_wait + sent + [own_over]:
        copy.wait_send()
    for own, away in out_waits:

        @pl.when(jnp.logical_not(own))
        def _():
            away.wait_send()


def per_device(out_grad, filter_mats, coeffs, pole_rates):
    dma = pltpu.SemaphoreType.DMA
    vmem = pl.BlockSpec(memory_space=pltpu.VMEM)
    return pl.pallas_call(
        kernel,
        out_shape=jax.ShapeDtypeStruct((TOK, WIDE), BF16),
        in_specs=[vmem] * 4,
        out_specs=vmem,
        scratch_shapes=[
            pltpu.VMEM((NX, ROWS, D), BF16),
            pltpu.VMEM((4, 2, 2, 128, D), BF16),
            pltpu.VMEM((TOK, D), BF16),
            pltpu.VMEM((TOK, D), BF16),
            pltpu.VMEM((D, 256), BF16),
            pltpu.VMEM((D, 256), BF16),
            pltpu.VMEM((4, 2, TOK, 128), F32),
            pltpu.VMEM((NY, TOK, WIDE), F32),
            pltpu.VMEM((TOK, 128), BF16),
            pltpu.VMEM((TOK, 128), BF16),
            pltpu.VMEM((128, 256), BF16),
            pltpu.VMEM((128, 256), BF16),
            pltpu.VMEM((4, 128, 128), F32),
            pltpu.VMEM((8, 128), F32),
            pltpu.VMEM((16, 128), F32),
            pltpu.VMEM((128, 128), F32),
            pltpu.VMEM((UNITS, 8, 128), F32),
            pltpu.VMEM((UNITS, 8, 128), F32),
            pltpu.VMEM((NZ, 3, 8, 128), F32),
            pltpu.VMEM((3, 8, 128), F32),
            pltpu.VMEM((NX, 3, 8, 128), F32),
            pltpu.VMEM((NZ, 3, 8, 128), F32),
            pltpu.VMEM((UNITS, 8, 128), F32),
            dma((2, 4)), dma((2, 4)), dma((2, 8)), dma((2, 8)),
            dma((2, 8)), dma((2, 16)), dma((2, 3)), dma((2, 3)),
            dma((17,)), dma((18,)),
            dma((16,)), dma((16,)), dma((17,)), dma((17,)),
            dma((NZ,)), dma((NZ,)), dma((NX,)), dma((NX,)), dma((NZ,)), dma((NZ,)),
            dma((16,)), dma((NY, 4)), dma((1,)),
        ],
        compiler_params=pltpu.CompilerParams(
            collective_id=0, has_side_effects=True, vmem_limit_bytes=60 * 1024 * 1024
        ),
        name="spectral_grad",
    )(out_grad, filter_mats, pole_rates.reshape(1, POLES), coeffs)


def solution(mesh):
    placed = (P("ctx", "grp"), P("grp", "ctx", None), P(), P())
    return jax.shard_map(
        per_device, mesh=mesh, in_specs=placed, out_specs=P("ctx", "grp"), check_vma=False
    )
```

```python
import jax
import jax.numpy as jnp
from jax import lax
from jax.experimental import pallas as pl
from jax.experimental.pallas import tpu as pltpu
from jax.sharding import PartitionSpec as P

MESH = pl.DeviceIdType.MESH
F32, BF16 = jnp.float32, jnp.bfloat16
NX, NZ, NY = 4, 8, 4
TOK, WIDE, HALF, D = 512, 256, 1024, 2048
POLES, UNITS = 80, 24
HI = TOK
LO = TOK + POLES
ROWS = TOK + 2 * POLES
NT = (((1,), (1,)), ((), ()))
NN = (((1,), (0,)), ((), ()))
OFFSETS = (0, -1, 1, 2)


def split(value):
    high = value.astype(BF16)
    return high, (value - high.astype(F32)).astype(BF16)


def mm(a, b, dims=NN):
    return lax.dot_general(a, b, dims, preferred_element_type=F32)


def minus_expm1_neg(u):
    series = jnp.ones_like(u)
    for n in range(9, 1, -1):
        series = 1.0 - u * (1.0 / n) * series
    return jnp.where(u < 0.25, u * series, 1.0 - jnp.exp(-u))


def kernel(
    g_ref, m_ref, rates_ref, coeffs_ref, out_ref,
    grads, mats, kern_hi, kern_lo, proj_hi, proj_lo, parts, arrived, edge_hi, edge_lo,
    state_hi, state_lo, coef_col, rates_row, coef_row, rates_col, unit_rates, unit_out, unit_in,
    total_out, total_in, enter_out, enter_in,
    p1_send, p1_recv, p2_send, p2_recv, rl_send, rl_recv, sh_send, sh_recv,
    g_send, g_recv, m_send, m_recv, ms_send, ms_recv, u_send, u_recv,
    t_send, t_recv, e_send, e_recv, o_send, o_recv, l_sem, near_sem,
):
    ctx, grp = lax.axis_index("ctx"), lax.axis_index("grp")
    x, z, y, c = ctx // NZ, ctx % NZ, grp // 2, grp % 2

    def device(x_to=None, z_to=None, y_to=None, c_to=None):
        pick = lambda new, own: own if new is None else new
        return (pick(x_to, x) * NZ + pick(z_to, z), pick(y_to, y) * 2 + pick(c_to, c))

    def remote(src, dst, send, recv, target):
        copy = pltpu.make_async_remote_copy(
            src_ref=src, dst_ref=dst, send_sem=send, recv_sem=recv,
            device_id=target, device_id_type=MESH,
        )
        return copy

    sibling = device(c_to=1 - c)
    slot = lambda x_of: (x_of + 4 - 2 * c) % NX
    col = lambda y_of: pl.ds(pl.multiple_of(c * HALF + y_of * WIDE, WIDE), WIDE)
    side = pl.ds(pl.multiple_of(c * HALF, HALF), HALF)

    barrier = pltpu.get_barrier_semaphore()
    partners = [device(z_to=(z + d) % NZ) for d in (1, NZ - 1)]
    partners += [device(x_to=(x + d) % NX) for d in (1, NX - 1)]
    partners += [device(y_to=(y + d) % NY) for d in (1, NY - 1)]
    partners += [sibling]
    for target in partners:
        pl.semaphore_signal(barrier, inc=1, device_id=target, device_id_type=MESH)

    low = pl.ds(pl.multiple_of(64 * (z % 2), 64), 64)
    for c_of in range(2):
        for y_of in range(NY):
            mats[z // 2, :, c, low, (c_of * NY + y_of) * WIDE : (c_of * NY + y_of + 1) * WIDE] = m_ref[
                :, :, (y_of * 2 + c_of) * WIDE : (y_of * 2 + c_of + 1) * WIDE
            ]
    own_copy = pltpu.make_async_copy(g_ref, grads.at[slot(x), 0:TOK, col(y)], l_sem.at[0])
    own_copy.start()

    rates_row[...] = jnp.zeros_like(rates_row)
    coef_row[...] = jnp.zeros_like(coef_row)
    rates_row[0:1, 0:POLES] = rates_ref[...]
    coef_row[:, 0:POLES] = coeffs_ref[...]
    rates_col[...] = jnp.broadcast_to(rates_row[0:1, :], (128, 128)).T
    gains = jnp.sqrt(minus_expm1_neg(2.0 * rates_row[0:1, :]))
    rates_c = rates_col[0:POLES, :]
    state = jnp.zeros((POLES, WIDE), F32)
    for part in range(4):
        pos = lax.broadcasted_iota(jnp.int32, (POLES, 128), 1).astype(F32) + 128.0 * part
        dec_hi, dec_lo = split(jnp.exp(-pos * rates_c))
        rows = g_ref[128 * part : 128 * part + 128, :]
        state = state + mm(dec_hi, rows) + mm(dec_lo, rows)
    for group in range(10):
        for half in range(2):
            unit_out[group * 2 + half] = state[8 * group : 8 * group + 8, 128 * half : 128 * half + 128]
            unit_rates[group * 2 + half] = rates_col[8 * group : 8 * group + 8, :]

    pl.semaphore_wait(barrier, len(partners))

    def piece(z_of, d, k, way):
        start, size = 64 * (z_of % 2), 64
        if d == 4:
            start, size = start + 16 * (1 - way), 32
        return mats.at[z_of // 2, k, c, pl.ds(pl.multiple_of(start, 32), size), :]

    m_wait, ms_wait = [], []

    def ring(d, k, way):
        z_of = (z + NZ - way * (d - 1)) % NZ
        ref = piece(z_of, d, k, way)
        i = ((d - 1) * 2 + k) * 2 + (way + 1) // 2
        copy = remote(ref, ref, m_send.at[i], m_recv.at[i], device(z_to=(z + NZ + way) % NZ))
        copy.start()
        m_wait.append(copy)
        return copy

    def arrive(copy, d, k, way):
        z_of = (z + NZ - way * d) % NZ
        ref = piece(z_of, d, k, way)
        i = ((d - 1) * 2 + k) * 2 + (way + 1) // 2
        copy.wait_recv()
        over = remote(ref, ref, ms_send.at[i], ms_recv.at[i], sibling)
        over.start()
        ms_wait.append(over)
        return over

    ring_copies, over_copies = {}, {}

    def event(d, k):
        for way in (1, -1):
            over_copies[d, k, way] = arrive(ring_copies[d, k, way], d, k, way)
            if d < 4:
                ring_copies[d + 1, k, way] = ring(d + 1, k, way)

    for way in (1, -1):
        ring_copies[1, 0, way] = ring(1, 0, way)
    for step in range(3):
        for d in (1, NZ - 1):
            pl.semaphore_signal(
                near_sem.at[step], inc=1, device_id=device(z_to=(z + d) % NZ), device_id_type=MESH
            )
        pl.semaphore_wait(near_sem.at[step], 2)
    unit_copies = []
    for d in range(1, NZ):
        to = (z + d) % NZ
        copy = remote(
            unit_out.at[pl.ds(3 * to, 3)], unit_in.at[z], u_send.at[d], u_recv.at[d], device(z_to=to)
        )
        copy.start()
        unit_copies.append(copy)

    g_wait, sent = [], []

    def send_g(i, j, src, dst, target):
        copy = remote(src, dst, g_send.at[i], g_recv.at[j], target)
        copy.start()
        g_wait.append(copy)

    north = lambda d: (y + NY + d) % NY
    east = lambda d: (x + NX + d) % NX
    to_y = lambda d: device(y_to=north(d))
    to_x = lambda d: device(x_to=east(d))

    hi_rows, lo_rows = pl.ds(HI, POLES), pl.ds(LO, POLES)

    def states_first():
        for d in range(1, 4):
            ref = grads.at[slot(x), hi_rows, col(y)]
            send_g(d - 1, d - 1, ref, ref, to_y(d))
            ref = grads.at[slot(x), lo_rows, col(y)]
            send_g(3 + d - 1, 3 + d - 1, ref, ref, to_x(d))

    def states_second():
        for copy in g_wait[0:6]:
            copy.wait_recv()
        ref, dst = grads.at[slot(x), hi_rows, side], grads.at[x % 2, hi_rows, side]
        for d in range(1, 4):
            send_g(6 + d - 1, 6 + 2 * (x % 2) + c, ref, dst, device(x_to=east(d), c_to=x // 2))
        hi_over = remote(ref, dst, g_send.at[9], g_recv.at[6 + 2 * (x % 2) + c], sibling)

        @pl.when(x // 2 != c)
        def _():
            hi_over.start()

        dst = grads.at[0:2, lo_rows, col(y)]
        away = grads.at[2:4, lo_rows, col(y)]
        for d in range(1, 4):
            send_g(9 + d, 10 + 2 * y + c, dst, dst, to_y(d))
            send_g(12 + d, 10 + 2 * y + c, away, dst, device(y_to=north(d), c_to=1 - c))
        send_g(16, 10 + 2 * y + c, away, dst, sibling)
        return hi_over

    def states_finish():
        ref = grads.at[0, hi_rows, side]
        for b in range(2):
            for c_of in range(2):

                @pl.when(jnp.logical_not(jnp.logical_and(2 * c + b == x, c_of == c)))
                def _():
                    remote(ref, ref, g_send.at[0], g_recv.at[6 + 2 * b + c_of], sibling).wait_recv()

        ref2 = grads.at[0:2, lo_rows, col(y)]
        for y_of in range(NY):
            for c_of in range(2):

                @pl.when(jnp.logical_not(jnp.logical_and(y_of == y, c_of == c)))
                def _():
                    remote(ref2, ref2, g_send.at[0], g_recv.at[10 + 2 * y_of + c_of], sibling).wait_recv()

    class Tokens:
        def __init__(self, n, row, y_first):
            self.n, self.y_first = n, y_first
            self.rows, self.first, self.last = pl.ds(row, 256), pl.ds(row, 128), pl.ds(row + 128, 128)
            self.src = g_ref.at[row : row + 256, :]
            self.hop1, self.hop2 = (to_y, to_x) if y_first else (to_x, to_y)
            self.p1, self.p2, self.shares = {}, {}, []

        def ref(self, d1, d2, rows, s=None):
            dx, dy = (d2, d1) if self.y_first else (d1, d2)
            return grads.at[slot(east(dx)) if s is None else s, rows, col(north(dy))]

        def copy(self, src, dst, i, target, first=True):
            send, recv = (p1_send, p1_recv) if first else (p2_send, p2_recv)
            copy = remote(src, dst, send.at[self.n, i], recv.at[self.n, i], target)
            copy.start()
            sent.append(copy)
            return copy

        def onward(self, j, src=None):
            ref = self.ref(OFFSETS[j], 0, self.rows)
            for way in (1, -1):
                self.p2[j, way] = self.copy(
                    ref if src is None else src, ref, 2 * j + (way + 1) // 2, self.hop2(way), False
                )

        def start(self):
            halves = ((self.first, self.src.at[0:128, :]), (self.last, self.src.at[128:256, :]))
            for i in range(2):
                for at, way in ((0, 1), (1, -1)):
                    rows, src = halves[i ^ at]
                    self.p1[at, i] = self.copy(src, self.ref(0, 0, rows), 2 * i + at, self.hop1(way))

        def mid(self):
            for i, way, rows in ((0, 1, self.first), (1, -1, self.last)):
                self.p1[i, 0].wait_recv()
                ref = self.ref(-way, 0, rows)
                self.p1[i, 2] = self.copy(ref, ref, i + 4, self.hop1(way))

        def opposite(self):
            self.p1[0, 2].wait_recv()
            self.p1[1, 2].wait_recv()
            self.onward(3)

        def relay(self, j):
            for way, rows in ((1, self.first), (-1, self.last)):
                self.p2[j, way].wait_recv()
                owner = east(-way) if self.y_first else east(OFFSETS[j])
                at = 8 * c + 2 * j + (way + 1) // 2 if self.y_first else 4 * c + 2 * (owner % 2) + (way + 1) // 2
                target = (
                    device(x_to=east(way), c_to=owner // 2)
                    if self.y_first
                    else device(y_to=north(way), c_to=owner // 2)
                )
                copy = remote(
                    self.ref(OFFSETS[j], -way, rows), self.ref(OFFSETS[j], -way, rows, owner % 2),
                    rl_send.at[self.n, 2 * j + (way + 1) // 2], rl_recv.at[self.n, at], target,
                )
                copy.start()
                sent.append(copy)

        def share_copy(self, i, src, dst):
            return remote(src, dst, sh_send.at[self.n, i], sh_recv.at[self.n, i], sibling)

        def share(self):
            if self.y_first:
                mine = x // 2 == 1 - c
                buddy = lambda v: v + 1 - 2 * (v % 2)
                s0 = slot(jnp.where(mine, x, buddy(east(2))))
                s1 = slot(jnp.where(mine, buddy(x), x))
                at = lambda s: grads.at[s, self.rows, side]
                copy = self.share_copy(0, at(s0), at(s0 - 2))
                copy.start()
                sent.append(copy)
                self.shares.append(copy)
                self.extra = self.share_copy(1, at(jnp.where(mine, s1, 2)), at(jnp.where(mine, s1 - 2, 0)))

                @pl.when(mine)
                def _():
                    self.extra.start()
            else:
                for i, dy in enumerate((0, -1, 1)):
                    at = lambda lo: grads.at[lo : lo + 2, self.rows, col(north(dy))]
                    copy = self.share_copy(i, at(2), at(0))
                    copy.start()
                    sent.append(copy)
                    self.shares.append(copy)

        def finish(self):
            for copy in self.shares:
                copy.wait_recv()
            piece_ref = grads.at[0, self.first, 0:WIDE]

            def wait_relays(count):
                for at in range(count):
                    remote(
                        piece_ref, piece_ref, rl_send.at[self.n, 0], rl_recv.at[self.n, at], sibling
                    ).wait_recv()

            if self.y_first:

                @pl.when(x // 2 == c)
                def _():
                    self.extra.wait_recv()

                @pl.when(east(2) // 2 == c)
                def _():
                    wait_relays(16)
            else:
                wait_relays(8)

        def drain(self):
            if self.y_first:

                @pl.when(x // 2 == 1 - c)
                def _():
                    self.extra.wait_send()

    tok_a, tok_b = Tokens(0, 0, True), Tokens(1, 256, False)

    tok_a.start()
    tok_b.start()

    tok_a.onward(0, tok_a.src)
    tok_b.onward(0, tok_b.src)
    for way in (1, -1):
        ring_copies[1, 1, way] = ring(1, 1, way)
    own_ref = mats.at[z // 2, :, c, low, :]
    own_over = remote(own_ref, own_ref, ms_send.at[16], ms_recv.at[16], sibling)
    own_over.start()

    own_units = pl.ds(3 * z, 3)
    total_copies, enter_copies = [], []

    def hand_on():
        lam = jnp.exp(-float(TOK) * unit_rates[own_units])
        unit_in[z] = unit_out[own_units]
        for copy in unit_copies:
            copy.wait_recv()
        run = jnp.zeros((3, 8, 128), F32)
        for z_of in range(NZ - 1, -1, -1):
            enter_out[z_of] = run
            run = unit_in[z_of] + lam * run
        total_out[...] = run
        total_in[x] = run
        for d in range(1, NX):
            copy = remote(
                total_out, total_in.at[x], t_send.at[d], t_recv.at[d], device(x_to=(x + d) % NX)
            )
            copy.start()
            total_copies.append(copy)

    def send_enter():
        for copy in total_copies:
            copy.wait_recv()
        lam_row = jnp.exp(-float(TOK * NZ) * unit_rates[own_units])
        carry = jnp.zeros((3, 8, 128), F32)
        for x_of in range(NX - 1, 0, -1):
            carry = jnp.where(x_of > x, total_in[x_of] + lam_row * carry, carry)
        lam = jnp.exp(-float(TOK) * unit_rates[own_units])
        for z_of in range(NZ - 1, -1, -1):
            enter_out[z_of] = enter_out[z_of] + carry
            carry = lam * carry
        for d in range(1, NZ):
            to = (z + d) % NZ
            copy = remote(
                enter_out.at[to], enter_in.at[own_units], e_send.at[d], e_recv.at[d], device(z_to=to)
            )
            copy.start()
            enter_copies.append(copy)
        enter_in[own_units] = enter_out[z]

    def store_enter():
        for d in range(1, NZ):
            source = (z + NZ - d) % NZ
            remote(
                enter_out.at[0], enter_in.at[pl.ds(3 * source, 3)], e_send.at[d], e_recv.at[d], sibling
            ).wait_recv()
        for group in range(10):
            for half in range(2):
                high, rest = split(enter_in[group * 2 + half])
                grads_cols = pl.ds(pl.multiple_of(c * HALF + y * WIDE + 128 * half, 128), 128)
                grads[slot(x), HI + 8 * group : HI + 8 * group + 8, grads_cols] = high
                grads[slot(x), LO + 8 * group : LO + 8 * group + 8, grads_cols] = rest

    rates_r = rates_row[0:1, :]
    rise_pos = lax.broadcasted_iota(jnp.int32, (TOK, 128), 0).astype(F32)
    falling = jnp.exp((rise_pos - 256.0) * rates_r)
    rising = jnp.exp((256.0 - rise_pos) * rates_r)
    edge = gains * jnp.exp((rise_pos - float(TOK)) * rates_r)
    edge_hi[...], edge_lo[...] = split(edge)

    def taps(th, k):
        size = 256 * (th + 1)
        scaled = rising[256 * th : 256 * th + 256] * (coef_row[pl.ds(4 * y + k, 1), :] * gains)
        mat = lax.dot_general(
            falling[0:size], scaled, NT, precision=lax.Precision.HIGHEST, preferred_element_type=F32
        )
        s_at = lax.broadcasted_iota(jnp.int32, (size, 256), 0)
        t_at = lax.broadcasted_iota(jnp.int32, (size, 256), 1) + 256 * th
        high, rest = split(jnp.where(t_at >= s_at, mat, 0.0))
        at = (k % 2) * HALF + th * TOK + (k // 2) * 256
        kern_hi[0:size, at : at + 256] = high
        kern_lo[0:size, at : at + 256] = rest

    def more_taps(ks):
        for k in ks:
            taps(1, k)
            coef_col[k] = jnp.broadcast_to(coef_row[pl.ds(4 * y + k, 1), :], (128, 128)).T

    tok_a.mid()
    tok_b.mid()
    hand_on()
    for j in (1, 2):
        tok_a.p1[j - 1, 1].wait_recv()
        tok_a.onward(j)
        tok_b.p1[j - 1, 1].wait_recv()
        tok_b.onward(j)
    for k in range(4):
        taps(0, k)
    own_copy.wait()
    tok_a.opposite()
    tok_b.opposite()
    send_enter()
    event(1, 0)
    tok_a.relay(0)
    tok_b.relay(0)
    more_taps((0, 1))
    tok_a.relay(1)
    tok_b.relay(1)
    event(1, 1)
    tok_a.relay(2)
    tok_b.relay(2)
    state_hi[...] = jnp.zeros_like(state_hi)
    state_lo[...] = jnp.zeros_like(state_lo)
    store_enter()
    tok_a.relay(3)
    tok_b.relay(3)
    states_first()
    tok_a.share()
    tok_b.share()
    more_taps((2,))
    event(2, 0)
    more_taps((3,))

    def project(q, kk, ths=(0, 1)):
        weights = mats[q, kk].reshape(256, D)
        parts_of = [(block, th) for block in range(2) for th in ths]
        tiles = [mm(grads[block, 256 * th : 256 * th + 256, :], weights, NT) for block, th in parts_of]
        for (block, th), tile in zip(parts_of, tiles):
            high, rest = split(tile)
            for c_of in range(2):
                at = kk * HALF + th * TOK + c_of * 256
                lanes, own = slice(128 * block, 128 * block + 128), slice(128 * c_of, 128 * c_of + 128)
                proj_hi[at : at + 256, lanes] = high[:, own]
                proj_lo[at : at + 256, lanes] = rest[:, own]

    def near(sh, kk):
        s_rows = slice(256 * sh, 256 * sh + 256)
        t_rows = slice(HALF * kk + TOK * sh, HALF * kk + HALF)
        return (
            mm(kern_hi[s_rows, t_rows], proj_hi[t_rows, :])
            + mm(kern_hi[s_rows, t_rows], proj_lo[t_rows, :])
            + mm(kern_lo[s_rows, t_rows], proj_hi[t_rows, :])
        )

    def enter(q):
        both = mm(grads[0:2, HI:ROWS, :].reshape(4 * POLES, D), mats[q].reshape(512, D), NT)
        for block in range(2):
            total = jnp.zeros((POLES, 128), F32)
            top = 2 * POLES * block
            for kk in range(2):
                for c_of in range(2):
                    at = 256 * kk + 128 * c_of
                    lanes = slice(at, at + 128)
                    total = total + coef_col[2 * c_of + kk, 0:POLES, :] * (
                        both[top : top + POLES, lanes] + both[top + POLES : top + 2 * POLES, lanes]
                    )
            high, rest = split(total)
            state_hi[0:POLES, 128 * block : 128 * block + 128] = high
            state_lo[0:POLES, 128 * block : 128 * block + 128] = rest

    def far(sh):
        s_rows = slice(256 * sh, 256 * sh + 256)
        return (
            mm(edge_hi[s_rows, :], state_hi[...])
            + mm(edge_hi[s_rows, :], state_lo[...])
            + mm(edge_lo[s_rows, :], state_hi[...])
        )

    out_waits = []

    def deliver(n, q, sh):
        s_rows = slice(256 * sh, 256 * sh + 256)
        for block in range(2):
            own = jnp.logical_and(jnp.logical_and(2 * c + block == x, x == y), q // 2 == c)
            cols = pl.ds(pl.multiple_of((q % 2) * 128, 128), 128)
            src, dst = parts.at[n, block, s_rows, :], arrived.at[y, s_rows, cols]
            done = o_recv.at[y, 2 * (q % 2) + sh]
            away = remote(
                src, dst, o_send.at[4 * n + 2 * block + sh], done,
                device(x_to=2 * c + block, y_to=x, c_to=q // 2),
            )
            local = pltpu.make_async_copy(src, dst, done)

            @pl.when(jnp.logical_not(own))
            def _():
                away.start()

            @pl.when(own)
            def _():
                local.start()

            out_waits.append((own, away))

    def store(n, sh, value, add=False):
        s_rows = slice(256 * sh, 256 * sh + 256)
        for block in range(2):
            new = value[:, 128 * block : 128 * block + 128]
            parts[n, block, s_rows, :] = parts[n, block, s_rows, :] + new if add else new

    def over_in(d, k):
        for way in (1, -1):
            if (d, k, way) in over_copies:
                over_copies[d, k, way].wait_recv()

    q_own = z // 2
    lean = 1 - 2 * (z % 2)
    order = [q_own, (q_own + 4 - lean) % 4, (q_own + 4 + lean) % 4, (q_own + 2) % 4]

    own_over.wait_recv()
    over_in(1, 0)
    over_in(1, 1)
    tok_a.finish()
    tok_b.finish()
    hi_over = states_second()
    project(order[0], 0)
    project(order[0], 1)
    event(2, 1)
    for sh in range(2):
        store(0, sh, near(sh, 0) + near(sh, 1))
    over_in(2, 0)
    over_in(2, 1)
    project(order[1], 0)
    event(3, 0)
    project(order[1], 1)
    states_finish()
    enter(order[0])
    for sh in range(2):
        store(0, sh, far(sh), True)
        deliver(0, order[0], sh)
    enter(order[1])
    for sh in (1, 0):
        store(1, sh, near(sh, 0) + near(sh, 1) + far(sh))
        deliver(1, order[1], sh)
    event(3, 1)
    over_in(3, 0)
    project(order[2], 0)
    for sh in range(2):
        store(2, sh, near(sh, 0))
    event(4, 0)
    over_in(3, 1)
    project(order[2], 1)
    enter(order[2])
    for sh in (1, 0):
        store(2, sh, near(sh, 1) + far(sh), True)
        deliver(2, order[2], sh)
    event(4, 1)
    over_in(4, 0)
    project(order[3], 0)
    for sh in range(2):
        store(3, sh, near(sh, 0))
    over_in(4, 1)
    enter(order[3])
    for sh in (1, 0):
        project(order[3], 1, (sh,))
        store(3, sh, near(sh, 1) + far(sh), True)
        deliver(3, order[3], sh)

    for n in range(4):
        q = order[n]

        @pl.when(q // 2 == c)
        def _():
            cols = pl.ds(pl.multiple_of((q % 2) * 128, 128), 128)
            for sh in (1, 0):
                s_rows = slice(256 * sh, 256 * sh + 256)
                for y_of in range(NY):
                    ref = arrived.at[y_of, s_rows, cols]
                    pltpu.make_async_copy(ref, ref, o_recv.at[y_of, 2 * (q % 2) + sh]).wait()
                total = arrived[0, s_rows, cols] + arrived[1, s_rows, cols]
                total = total + arrived[2, s_rows, cols] + arrived[3, s_rows, cols]
                out_ref[s_rows, cols] = total.astype(BF16)

    tok_a.drain()

    @pl.when(x // 2 != c)
    def _():
        hi_over.wait_send()

    for copy in unit_copies + total_copies + enter_copies + m_wait + ms_wait + g_wait + sent + [own_over]:
        copy.wait_send()
    for own, away in out_waits:

        @pl.when(jnp.logical_not(own))
        def _():
            away.wait_send()


def per_device(out_grad, filter_mats, coeffs, pole_rates):
    dma = pltpu.SemaphoreType.DMA
    vmem = pl.BlockSpec(memory_space=pltpu.VMEM)
    return pl.pallas_call(
        kernel,
        out_shape=jax.ShapeDtypeStruct((TOK, WIDE), BF16),
        in_specs=[vmem] * 4,
        out_specs=vmem,
        scratch_shapes=[
            pltpu.VMEM((NX, ROWS, D), BF16),
            pltpu.VMEM((4, 2, 2, 128, D), BF16),
            pltpu.VMEM((TOK, D), BF16),
            pltpu.VMEM((TOK, D), BF16),
            pltpu.VMEM((D, 256), BF16),
            pltpu.VMEM((D, 256), BF16),
            pltpu.VMEM((4, 2, TOK, 128), F32),
            pltpu.VMEM((NY, TOK, WIDE), F32),
            pltpu.VMEM((TOK, 128), BF16),
            pltpu.VMEM((TOK, 128), BF16),
            pltpu.VMEM((128, 256), BF16),
            pltpu.VMEM((128, 256), BF16),
            pltpu.VMEM((4, 128, 128), F32),
            pltpu.VMEM((8, 128), F32),
            pltpu.VMEM((16, 128), F32),
            pltpu.VMEM((128, 128), F32),
            pltpu.VMEM((UNITS, 8, 128), F32),
            pltpu.VMEM((UNITS, 8, 128), F32),
            pltpu.VMEM((NZ, 3, 8, 128), F32),
            pltpu.VMEM((3, 8, 128), F32),
            pltpu.VMEM((NX, 3, 8, 128), F32),
            pltpu.VMEM((NZ, 3, 8, 128), F32),
            pltpu.VMEM((UNITS, 8, 128), F32),
            dma((2, 6)), dma((2, 6)), dma((2, 8)), dma((2, 8)),
            dma((2, 8)), dma((2, 16)), dma((2, 3)), dma((2, 3)),
            dma((17,)), dma((18,)),
            dma((16,)), dma((16,)), dma((17,)), dma((17,)),
            dma((NZ,)), dma((NZ,)), dma((NX,)), dma((NX,)), dma((NZ,)), dma((NZ,)),
            dma((16,)), dma((NY, 4)), dma((1,)), pltpu.SemaphoreType.REGULAR((3,)),
        ],
        compiler_params=pltpu.CompilerParams(
            collective_id=0, has_side_effects=True, vmem_limit_bytes=60 * 1024 * 1024
        ),
        name="spectral_grad",
    )(out_grad, filter_mats, pole_rates.reshape(1, POLES), coeffs)


def solution(mesh):
    placed = (P("ctx", "grp"), P("grp", "ctx", None), P(), P())
    return jax.shard_map(
        per_device, mesh=mesh, in_specs=placed, out_specs=P("ctx", "grp"), check_vma=False
    )
```

```python
import jax
import jax.numpy as jnp
from jax import lax
from jax.experimental import pallas as pl
from jax.experimental.pallas import tpu as pltpu
from jax.sharding import PartitionSpec as P

MESH = pl.DeviceIdType.MESH
F32, BF16 = jnp.float32, jnp.bfloat16
NX, NZ, NY = 4, 8, 4
TOK, WIDE, HALF, D = 512, 256, 1024, 2048
POLES, UNITS = 80, 24
HI = TOK
LO = TOK + POLES
ROWS = TOK + 2 * POLES
NT = (((1,), (1,)), ((), ()))
NN = (((1,), (0,)), ((), ()))
OFFSETS = (0, -1, 1, 2)


def split(value):
    high = value.astype(BF16)
    return high, (value - high.astype(F32)).astype(BF16)


def mm(a, b, dims=NN):
    return lax.dot_general(a, b, dims, preferred_element_type=F32)


def minus_expm1_neg(u):
    series = jnp.ones_like(u)
    for n in range(9, 1, -1):
        series = 1.0 - u * (1.0 / n) * series
    return jnp.where(u < 0.25, u * series, 1.0 - jnp.exp(-u))


def kernel(
    g_hbm, m_hbm, rates_hbm, coeffs_hbm, out_ref,
    g_ref, rates_ref, coeffs_ref, grads, mats, kern_hi, kern_lo, proj_hi, proj_lo, parts, arrived, edge_hi, edge_lo,
    state_hi, state_lo, coef_col, rates_row, coef_row, rates_col, unit_rates, unit_out, unit_in,
    total_out, total_in, enter_out, enter_in,
    p1_send, p1_recv, p2_send, p2_recv, rl_send, rl_recv, sh_send, sh_recv,
    g_send, g_recv, m_send, m_recv, ms_send, ms_recv, u_send, u_recv,
    t_send, t_recv, e_send, e_recv, o_send, o_recv, l_sem, i_sem, near_sem,
):
    ctx, grp = lax.axis_index("ctx"), lax.axis_index("grp")
    x, z, y, c = ctx // NZ, ctx % NZ, grp // 2, grp % 2

    def device(x_to=None, z_to=None, y_to=None, c_to=None):
        pick = lambda new, own: own if new is None else new
        return (pick(x_to, x) * NZ + pick(z_to, z), pick(y_to, y) * 2 + pick(c_to, c))

    def remote(src, dst, send, recv, target):
        copy = pltpu.make_async_remote_copy(
            src_ref=src, dst_ref=dst, send_sem=send, recv_sem=recv,
            device_id=target, device_id_type=MESH,
        )
        return copy

    sibling = device(c_to=1 - c)
    slot = lambda x_of: (x_of + 4 - 2 * c) % NX
    col = lambda y_of: pl.ds(pl.multiple_of(c * HALF + y_of * WIDE, WIDE), WIDE)
    side = pl.ds(pl.multiple_of(c * HALF, HALF), HALF)

    barrier = pltpu.get_barrier_semaphore()
    partners = [device(z_to=(z + d) % NZ) for d in (1, NZ - 1)]
    partners += [device(x_to=(x + d) % NX) for d in (1, NX - 1)]
    partners += [device(y_to=(y + d) % NY) for d in (1, NY - 1)]
    partners += [sibling]
    for target in partners:
        pl.semaphore_signal(barrier, inc=1, device_id=target, device_id_type=MESH)

    low = pl.ds(pl.multiple_of(64 * (z % 2), 64), 64)
    fetches = [
        pltpu.make_async_copy(rates_hbm, rates_ref, i_sem.at[0]),
        pltpu.make_async_copy(coeffs_hbm, coeffs_ref, i_sem.at[1]),
        pltpu.make_async_copy(g_hbm, g_ref, i_sem.at[2]),
    ]
    for c_of in range(2):
        for y_of in range(NY):
            to, at = (c_of * NY + y_of) * WIDE, (y_of * 2 + c_of) * WIDE
            fetches.append(
                pltpu.make_async_copy(
                    m_hbm.at[:, :, at : at + WIDE],
                    mats.at[z // 2, :, c, low, to : to + WIDE],
                    i_sem.at[3 + c_of * NY + y_of],
                )
            )
    for fetch in fetches:
        fetch.start()
    for fetch in fetches[0:3]:
        fetch.wait()
    own_copy = pltpu.make_async_copy(g_ref, grads.at[slot(x), 0:TOK, col(y)], l_sem.at[0])
    own_copy.start()

    rates_row[...] = jnp.zeros_like(rates_row)
    coef_row[...] = jnp.zeros_like(coef_row)
    rates_row[0:1, 0:POLES] = rates_ref[...]
    coef_row[:, 0:POLES] = coeffs_ref[...]
    rates_col[...] = jnp.broadcast_to(rates_row[0:1, :], (128, 128)).T
    gains = jnp.sqrt(minus_expm1_neg(2.0 * rates_row[0:1, :]))
    rates_c = rates_col[0:POLES, :]
    state = jnp.zeros((POLES, WIDE), F32)
    for part in range(4):
        pos = lax.broadcasted_iota(jnp.int32, (POLES, 128), 1).astype(F32) + 128.0 * part
        dec_hi, dec_lo = split(jnp.exp(-pos * rates_c))
        rows = g_ref[128 * part : 128 * part + 128, :]
        state = state + mm(dec_hi, rows) + mm(dec_lo, rows)
    for group in range(10):
        for half in range(2):
            unit_out[group * 2 + half] = state[8 * group : 8 * group + 8, 128 * half : 128 * half + 128]
            unit_rates[group * 2 + half] = rates_col[8 * group : 8 * group + 8, :]

    for fetch in fetches[3:]:
        fetch.wait()
    pl.semaphore_wait(barrier, len(partners))

    def piece(z_of, d, k, way):
        start, size = 64 * (z_of % 2), 64
        if d == 4:
            start, size = start + 16 * (1 - way), 32
        return mats.at[z_of // 2, k, c, pl.ds(pl.multiple_of(start, 32), size), :]

    m_wait, ms_wait = [], []

    def ring(d, k, way):
        z_of = (z + NZ - way * (d - 1)) % NZ
        ref = piece(z_of, d, k, way)
        i = ((d - 1) * 2 + k) * 2 + (way + 1) // 2
        copy = remote(ref, ref, m_send.at[i], m_recv.at[i], device(z_to=(z + NZ + way) % NZ))
        copy.start()
        m_wait.append(copy)
        return copy

    def arrive(copy, d, k, way):
        z_of = (z + NZ - way * d) % NZ
        ref = piece(z_of, d, k, way)
        i = ((d - 1) * 2 + k) * 2 + (way + 1) // 2
        copy.wait_recv()
        over = remote(ref, ref, ms_send.at[i], ms_recv.at[i], sibling)
        over.start()
        ms_wait.append(over)
        return over

    ring_copies, over_copies = {}, {}

    def event(d, k):
        for way in (1, -1):
            over_copies[d, k, way] = arrive(ring_copies[d, k, way], d, k, way)
            if d < 4:
                ring_copies[d + 1, k, way] = ring(d + 1, k, way)

    for way in (1, -1):
        ring_copies[1, 0, way] = ring(1, 0, way)
    for step in range(3):
        for d in (1, NZ - 1):
            pl.semaphore_signal(
                near_sem.at[step], inc=1, device_id=device(z_to=(z + d) % NZ), device_id_type=MESH
            )
        pl.semaphore_wait(near_sem.at[step], 2)
    unit_copies = []
    for d in range(1, NZ):
        to = (z + d) % NZ
        copy = remote(
            unit_out.at[pl.ds(3 * to, 3)], unit_in.at[z], u_send.at[d], u_recv.at[d], device(z_to=to)
        )
        copy.start()
        unit_copies.append(copy)

    g_wait, sent = [], []

    def send_g(i, j, src, dst, target):
        copy = remote(src, dst, g_send.at[i], g_recv.at[j], target)
        copy.start()
        g_wait.append(copy)

    north = lambda d: (y + NY + d) % NY
    east = lambda d: (x + NX + d) % NX
    to_y = lambda d: device(y_to=north(d))
    to_x = lambda d: device(x_to=east(d))

    hi_rows, lo_rows = pl.ds(HI, POLES), pl.ds(LO, POLES)

    def states_first():
        for d in range(1, 4):
            ref = grads.at[slot(x), hi_rows, col(y)]
            send_g(d - 1, d - 1, ref, ref, to_y(d))
            ref = grads.at[slot(x), lo_rows, col(y)]
            send_g(3 + d - 1, 3 + d - 1, ref, ref, to_x(d))

    def states_second():
        for copy in g_wait[0:6]:
            copy.wait_recv()
        ref, dst = grads.at[slot(x), hi_rows, side], grads.at[x % 2, hi_rows, side]
        for d in range(1, 4):
            send_g(6 + d - 1, 6 + 2 * (x % 2) + c, ref, dst, device(x_to=east(d), c_to=x // 2))
        hi_over = remote(ref, dst, g_send.at[9], g_recv.at[6 + 2 * (x % 2) + c], sibling)

        @pl.when(x // 2 != c)
        def _():
            hi_over.start()

        dst = grads.at[0:2, lo_rows, col(y)]
        away = grads.at[2:4, lo_rows, col(y)]
        for d in range(1, 4):
            send_g(9 + d, 10 + 2 * y + c, dst, dst, to_y(d))
            send_g(12 + d, 10 + 2 * y + c, away, dst, device(y_to=north(d), c_to=1 - c))
        send_g(16, 10 + 2 * y + c, away, dst, sibling)
        return hi_over

    def states_finish():
        ref = grads.at[0, hi_rows, side]
        for b in range(2):
            for c_of in range(2):

                @pl.when(jnp.logical_not(jnp.logical_and(2 * c + b == x, c_of == c)))
                def _():
                    remote(ref, ref, g_send.at[0], g_recv.at[6 + 2 * b + c_of], sibling).wait_recv()

        ref2 = grads.at[0:2, lo_rows, col(y)]
        for y_of in range(NY):
            for c_of in range(2):

                @pl.when(jnp.logical_not(jnp.logical_and(y_of == y, c_of == c)))
                def _():
                    remote(ref2, ref2, g_send.at[0], g_recv.at[10 + 2 * y_of + c_of], sibling).wait_recv()

    class Tokens:
        def __init__(self, n, row, y_first):
            self.n, self.y_first = n, y_first
            self.rows, self.first, self.last = pl.ds(row, 256), pl.ds(row, 128), pl.ds(row + 128, 128)
            self.src = g_ref.at[row : row + 256, :]
            self.hop1, self.hop2 = (to_y, to_x) if y_first else (to_x, to_y)
            self.p1, self.p2, self.shares = {}, {}, []

        def ref(self, d1, d2, rows, s=None):
            dx, dy = (d2, d1) if self.y_first else (d1, d2)
            return grads.at[slot(east(dx)) if s is None else s, rows, col(north(dy))]

        def copy(self, src, dst, i, target, first=True):
            send, recv = (p1_send, p1_recv) if first else (p2_send, p2_recv)
            copy = remote(src, dst, send.at[self.n, i], recv.at[self.n, i], target)
            copy.start()
            sent.append(copy)
            return copy

        def onward(self, j, src=None):
            ref = self.ref(OFFSETS[j], 0, self.rows)
            for way in (1, -1):
                self.p2[j, way] = self.copy(
                    ref if src is None else src, ref, 2 * j + (way + 1) // 2, self.hop2(way), False
                )

        def start(self):
            halves = ((self.first, self.src.at[0:128, :]), (self.last, self.src.at[128:256, :]))
            for i in range(2):
                for at, way in ((0, 1), (1, -1)):
                    rows, src = halves[i ^ at]
                    self.p1[at, i] = self.copy(src, self.ref(0, 0, rows), 2 * i + at, self.hop1(way))

        def mid(self):
            for i, way, rows in ((0, 1, self.first), (1, -1, self.last)):
                self.p1[i, 0].wait_recv()
                ref = self.ref(-way, 0, rows)
                self.p1[i, 2] = self.copy(ref, ref, i + 4, self.hop1(way))

        def opposite(self):
            self.p1[0, 2].wait_recv()
            self.p1[1, 2].wait_recv()
            self.onward(3)

        def relay(self, j):
            for way, rows in ((1, self.first), (-1, self.last)):
                self.p2[j, way].wait_recv()
                owner = east(-way) if self.y_first else east(OFFSETS[j])
                at = 8 * c + 2 * j + (way + 1) // 2 if self.y_first else 4 * c + 2 * (owner % 2) + (way + 1) // 2
                target = (
                    device(x_to=east(way), c_to=owner // 2)
                    if self.y_first
                    else device(y_to=north(way), c_to=owner // 2)
                )
                copy = remote(
                    self.ref(OFFSETS[j], -way, rows), self.ref(OFFSETS[j], -way, rows, owner % 2),
                    rl_send.at[self.n, 2 * j + (way + 1) // 2], rl_recv.at[self.n, at], target,
                )
                copy.start()
                sent.append(copy)

        def share_copy(self, i, src, dst):
            return remote(src, dst, sh_send.at[self.n, i], sh_recv.at[self.n, i], sibling)

        def share(self):
            if self.y_first:
                mine = x // 2 == 1 - c
                buddy = lambda v: v + 1 - 2 * (v % 2)
                s0 = slot(jnp.where(mine, x, buddy(east(2))))
                s1 = slot(jnp.where(mine, buddy(x), x))
                at = lambda s: grads.at[s, self.rows, side]
                copy = self.share_copy(0, at(s0), at(s0 - 2))
                copy.start()
                sent.append(copy)
                self.shares.append(copy)
                self.extra = self.share_copy(1, at(jnp.where(mine, s1, 2)), at(jnp.where(mine, s1 - 2, 0)))

                @pl.when(mine)
                def _():
                    self.extra.start()
            else:
                for i, dy in enumerate((0, -1, 1)):
                    at = lambda lo: grads.at[lo : lo + 2, self.rows, col(north(dy))]
                    copy = self.share_copy(i, at(2), at(0))
                    copy.start()
                    sent.append(copy)
                    self.shares.append(copy)

        def finish(self):
            for copy in self.shares:
                copy.wait_recv()
            piece_ref = grads.at[0, self.first, 0:WIDE]

            def wait_relays(count):
                for at in range(count):
                    remote(
                        piece_ref, piece_ref, rl_send.at[self.n, 0], rl_recv.at[self.n, at], sibling
                    ).wait_recv()

            if self.y_first:

                @pl.when(x // 2 == c)
                def _():
                    self.extra.wait_recv()

                @pl.when(east(2) // 2 == c)
                def _():
                    wait_relays(16)
            else:
                wait_relays(8)

        def drain(self):
            if self.y_first:

                @pl.when(x // 2 == 1 - c)
                def _():
                    self.extra.wait_send()

    tok_a, tok_b = Tokens(0, 0, True), Tokens(1, 256, False)

    tok_a.start()
    tok_b.start()

    tok_a.onward(0, tok_a.src)
    tok_b.onward(0, tok_b.src)
    for way in (1, -1):
        ring_copies[1, 1, way] = ring(1, 1, way)
    own_ref = mats.at[z // 2, :, c, low, :]
    own_over = remote(own_ref, own_ref, ms_send.at[16], ms_recv.at[16], sibling)
    own_over.start()

    own_units = pl.ds(3 * z, 3)
    total_copies, enter_copies = [], []

    def hand_on():
        lam = jnp.exp(-float(TOK) * unit_rates[own_units])
        unit_in[z] = unit_out[own_units]
        for copy in unit_copies:
            copy.wait_recv()
        run = jnp.zeros((3, 8, 128), F32)
        for z_of in range(NZ - 1, -1, -1):
            enter_out[z_of] = run
            run = unit_in[z_of] + lam * run
        total_out[...] = run
        total_in[x] = run
        for d in range(1, NX):
            copy = remote(
                total_out, total_in.at[x], t_send.at[d], t_recv.at[d], device(x_to=(x + d) % NX)
            )
            copy.start()
            total_copies.append(copy)

    def send_enter():
        for copy in total_copies:
            copy.wait_recv()
        lam_row = jnp.exp(-float(TOK * NZ) * unit_rates[own_units])
        carry = jnp.zeros((3, 8, 128), F32)
        for x_of in range(NX - 1, 0, -1):
            carry = jnp.where(x_of > x, total_in[x_of] + lam_row * carry, carry)
        lam = jnp.exp(-float(TOK) * unit_rates[own_units])
        for z_of in range(NZ - 1, -1, -1):
            enter_out[z_of] = enter_out[z_of] + carry
            carry = lam * carry
        for d in range(1, NZ):
            to = (z + d) % NZ
            copy = remote(
                enter_out.at[to], enter_in.at[own_units], e_send.at[d], e_recv.at[d], device(z_to=to)
            )
            copy.start()
            enter_copies.append(copy)
        enter_in[own_units] = enter_out[z]

    def store_enter():
        for d in range(1, NZ):
            source = (z + NZ - d) % NZ
            remote(
                enter_out.at[0], enter_in.at[pl.ds(3 * source, 3)], e_send.at[d], e_recv.at[d], sibling
            ).wait_recv()
        for group in range(10):
            for half in range(2):
                high, rest = split(enter_in[group * 2 + half])
                grads_cols = pl.ds(pl.multiple_of(c * HALF + y * WIDE + 128 * half, 128), 128)
                grads[slot(x), HI + 8 * group : HI + 8 * group + 8, grads_cols] = high
                grads[slot(x), LO + 8 * group : LO + 8 * group + 8, grads_cols] = rest

    rates_r = rates_row[0:1, :]
    rise_pos = lax.broadcasted_iota(jnp.int32, (TOK, 128), 0).astype(F32)
    falling = jnp.exp((rise_pos - 256.0) * rates_r)
    rising = jnp.exp((256.0 - rise_pos) * rates_r)
    edge = gains * jnp.exp((rise_pos - float(TOK)) * rates_r)
    edge_hi[...], edge_lo[...] = split(edge)

    def taps(th, k):
        size = 256 * (th + 1)
        scaled = rising[256 * th : 256 * th + 256] * (coef_row[pl.ds(4 * y + k, 1), :] * gains)
        mat = lax.dot_general(
            falling[0:size], scaled, NT, precision=lax.Precision.HIGHEST, preferred_element_type=F32
        )
        s_at = lax.broadcasted_iota(jnp.int32, (size, 256), 0)
        t_at = lax.broadcasted_iota(jnp.int32, (size, 256), 1) + 256 * th
        high, rest = split(jnp.where(t_at >= s_at, mat, 0.0))
        at = (k % 2) * HALF + th * TOK + (k // 2) * 256
        kern_hi[0:size, at : at + 256] = high
        kern_lo[0:size, at : at + 256] = rest

    def more_taps(ks):
        for k in ks:
            taps(1, k)
            coef_col[k] = jnp.broadcast_to(coef_row[pl.ds(4 * y + k, 1), :], (128, 128)).T

    tok_a.mid()
    tok_b.mid()
    hand_on()
    for j in (1, 2):
        tok_a.p1[j - 1, 1].wait_recv()
        tok_a.onward(j)
        tok_b.p1[j - 1, 1].wait_recv()
        tok_b.onward(j)
    for k in range(4):
        taps(0, k)
    own_copy.wait()
    tok_a.opposite()
    tok_b.opposite()
    send_enter()
    event(1, 0)
    tok_a.relay(0)
    tok_b.relay(0)
    more_taps((0, 1))
    tok_a.relay(1)
    tok_b.relay(1)
    event(1, 1)
    tok_a.relay(2)
    tok_b.relay(2)
    state_hi[...] = jnp.zeros_like(state_hi)
    state_lo[...] = jnp.zeros_like(state_lo)
    store_enter()
    tok_a.relay(3)
    tok_b.relay(3)
    states_first()
    tok_a.share()
    tok_b.share()
    more_taps((2,))
    event(2, 0)
    more_taps((3,))

    def project(q, kk, ths=(0, 1)):
        weights = mats[q, kk].reshape(256, D)
        parts_of = [(block, th) for block in range(2) for th in ths]
        tiles = [mm(grads[block, 256 * th : 256 * th + 256, :], weights, NT) for block, th in parts_of]
        for (block, th), tile in zip(parts_of, tiles):
            high, rest = split(tile)
            for c_of in range(2):
                at = kk * HALF + th * TOK + c_of * 256
                lanes, own = slice(128 * block, 128 * block + 128), slice(128 * c_of, 128 * c_of + 128)
                proj_hi[at : at + 256, lanes] = high[:, own]
                proj_lo[at : at + 256, lanes] = rest[:, own]

    def near(sh, kk):
        s_rows = slice(256 * sh, 256 * sh + 256)
        t_rows = slice(HALF * kk + TOK * sh, HALF * kk + HALF)
        return (
            mm(kern_hi[s_rows, t_rows], proj_hi[t_rows, :])
            + mm(kern_hi[s_rows, t_rows], proj_lo[t_rows, :])
            + mm(kern_lo[s_rows, t_rows], proj_hi[t_rows, :])
        )

    def enter(q):
        both = mm(grads[0:2, HI:ROWS, :].reshape(4 * POLES, D), mats[q].reshape(512, D), NT)
        for block in range(2):
            total = jnp.zeros((POLES, 128), F32)
            top = 2 * POLES * block
            for kk in range(2):
                for c_of in range(2):
                    at = 256 * kk + 128 * c_of
                    lanes = slice(at, at + 128)
                    total = total + coef_col[2 * c_of + kk, 0:POLES, :] * (
                        both[top : top + POLES, lanes] + both[top + POLES : top + 2 * POLES, lanes]
                    )
            high, rest = split(total)
            state_hi[0:POLES, 128 * block : 128 * block + 128] = high
            state_lo[0:POLES, 128 * block : 128 * block + 128] = rest

    def far(sh):
        s_rows = slice(256 * sh, 256 * sh + 256)
        return (
            mm(edge_hi[s_rows, :], state_hi[...])
            + mm(edge_hi[s_rows, :], state_lo[...])
            + mm(edge_lo[s_rows, :], state_hi[...])
        )

    out_waits = []

    def deliver(n, q, sh):
        s_rows = slice(256 * sh, 256 * sh + 256)
        for block in range(2):
            own = jnp.logical_and(jnp.logical_and(2 * c + block == x, x == y), q // 2 == c)
            cols = pl.ds(pl.multiple_of((q % 2) * 128, 128), 128)
            src, dst = parts.at[n, block, s_rows, :], arrived.at[y, s_rows, cols]
            done = o_recv.at[y, 2 * (q % 2) + sh]
            away = remote(
                src, dst, o_send.at[4 * n + 2 * block + sh], done,
                device(x_to=2 * c + block, y_to=x, c_to=q // 2),
            )
            local = pltpu.make_async_copy(src, dst, done)

            @pl.when(jnp.logical_not(own))
            def _():
                away.start()

            @pl.when(own)
            def _():
                local.start()

            out_waits.append((own, away))

    def store(n, sh, value, add=False):
        s_rows = slice(256 * sh, 256 * sh + 256)
        for block in range(2):
            new = value[:, 128 * block : 128 * block + 128]
            parts[n, block, s_rows, :] = parts[n, block, s_rows, :] + new if add else new

    def over_in(d, k):
        for way in (1, -1):
            if (d, k, way) in over_copies:
                over_copies[d, k, way].wait_recv()

    q_own = z // 2
    lean = 1 - 2 * (z % 2)
    order = [q_own, (q_own + 4 - lean) % 4, (q_own + 4 + lean) % 4, (q_own + 2) % 4]

    own_over.wait_recv()
    over_in(1, 0)
    over_in(1, 1)
    tok_a.finish()
    tok_b.finish()
    hi_over = states_second()
    project(order[0], 0)
    project(order[0], 1)
    event(2, 1)
    for sh in range(2):
        store(0, sh, near(sh, 0) + near(sh, 1))
    over_in(2, 0)
    over_in(2, 1)
    project(order[1], 0)
    event(3, 0)
    project(order[1], 1)
    states_finish()
    enter(order[0])
    for sh in range(2):
        store(0, sh, far(sh), True)
        deliver(0, order[0], sh)
    enter(order[1])
    for sh in (1, 0):
        store(1, sh, near(sh, 0) + near(sh, 1) + far(sh))
        deliver(1, order[1], sh)
    event(3, 1)
    over_in(3, 0)
    project(order[2], 0)
    for sh in range(2):
        store(2, sh, near(sh, 0))
    event(4, 0)
    over_in(3, 1)
    project(order[2], 1)
    enter(order[2])
    for sh in (1, 0):
        store(2, sh, near(sh, 1) + far(sh), True)
        deliver(2, order[2], sh)
    event(4, 1)
    over_in(4, 0)
    project(order[3], 0)
    for sh in range(2):
        store(3, sh, near(sh, 0))
    over_in(4, 1)
    enter(order[3])
    for sh in (1, 0):
        project(order[3], 1, (sh,))
        store(3, sh, near(sh, 1) + far(sh), True)
        deliver(3, order[3], sh)

    for n in range(4):
        q = order[n]

        @pl.when(q // 2 == c)
        def _():
            cols = pl.ds(pl.multiple_of((q % 2) * 128, 128), 128)
            for sh in (1, 0):
                s_rows = slice(256 * sh, 256 * sh + 256)
                for y_of in range(NY):
                    ref = arrived.at[y_of, s_rows, cols]
                    pltpu.make_async_copy(ref, ref, o_recv.at[y_of, 2 * (q % 2) + sh]).wait()
                total = arrived[0, s_rows, cols] + arrived[1, s_rows, cols]
                total = total + arrived[2, s_rows, cols] + arrived[3, s_rows, cols]
                out_ref[s_rows, cols] = total.astype(BF16)

    tok_a.drain()

    @pl.when(x // 2 != c)
    def _():
        hi_over.wait_send()

    for copy in unit_copies + total_copies + enter_copies + m_wait + ms_wait + g_wait + sent + [own_over]:
        copy.wait_send()
    for own, away in out_waits:

        @pl.when(jnp.logical_not(own))
        def _():
            away.wait_send()


def per_device(out_grad, filter_mats, coeffs, pole_rates):
    held = (out_grad, filter_mats, pole_rates.reshape(1, POLES), coeffs)
    dma = pltpu.SemaphoreType.DMA
    vmem = pl.BlockSpec(memory_space=pltpu.VMEM)
    return pl.pallas_call(
        kernel,
        out_shape=jax.ShapeDtypeStruct((TOK, WIDE), BF16),
        in_specs=[pl.BlockSpec(memory_space=pltpu.MemorySpace.HBM)] * 4,
        out_specs=vmem,
        scratch_shapes=[
            pltpu.VMEM((TOK, WIDE), BF16),
            pltpu.VMEM((1, POLES), F32),
            pltpu.VMEM((16, POLES), F32),
            pltpu.VMEM((NX, ROWS, D), BF16),
            pltpu.VMEM((4, 2, 2, 128, D), BF16),
            pltpu.VMEM((TOK, D), BF16),
            pltpu.VMEM((TOK, D), BF16),
            pltpu.VMEM((D, 256), BF16),
            pltpu.VMEM((D, 256), BF16),
            pltpu.VMEM((4, 2, TOK, 128), F32),
            pltpu.VMEM((NY, TOK, WIDE), F32),
            pltpu.VMEM((TOK, 128), BF16),
            pltpu.VMEM((TOK, 128), BF16),
            pltpu.VMEM((128, 256), BF16),
            pltpu.VMEM((128, 256), BF16),
            pltpu.VMEM((4, 128, 128), F32),
            pltpu.VMEM((8, 128), F32),
            pltpu.VMEM((16, 128), F32),
            pltpu.VMEM((128, 128), F32),
            pltpu.VMEM((UNITS, 8, 128), F32),
            pltpu.VMEM((UNITS, 8, 128), F32),
            pltpu.VMEM((NZ, 3, 8, 128), F32),
            pltpu.VMEM((3, 8, 128), F32),
            pltpu.VMEM((NX, 3, 8, 128), F32),
            pltpu.VMEM((NZ, 3, 8, 128), F32),
            pltpu.VMEM((UNITS, 8, 128), F32),
            dma((2, 6)), dma((2, 6)), dma((2, 8)), dma((2, 8)),
            dma((2, 8)), dma((2, 16)), dma((2, 3)), dma((2, 3)),
            dma((17,)), dma((18,)),
            dma((16,)), dma((16,)), dma((17,)), dma((17,)),
            dma((NZ,)), dma((NZ,)), dma((NX,)), dma((NX,)), dma((NZ,)), dma((NZ,)),
            dma((16,)), dma((NY, 4)), dma((1,)), dma((11,)), pltpu.SemaphoreType.REGULAR((3,)),
        ],
        compiler_params=pltpu.CompilerParams(
            collective_id=0, has_side_effects=True, vmem_limit_bytes=44 * 1024 * 1024
        ),
        name="spectral_grad",
    )(*[pltpu.with_memory_space_constraint(v, pltpu.MemorySpace.HBM) for v in held])


def solution(mesh):
    placed = (P("ctx", "grp"), P("grp", "ctx", None), P(), P())
    return jax.shard_map(
        per_device, mesh=mesh, in_specs=placed, out_specs=P("ctx", "grp"), check_vma=False
    )
```

```python
import jax
import jax.numpy as jnp
from jax import lax
from jax.experimental import pallas as pl
from jax.experimental.pallas import tpu as pltpu
from jax.sharding import PartitionSpec as P

MESH = pl.DeviceIdType.MESH
F32, BF16 = jnp.float32, jnp.bfloat16
NX, NZ, NY = 4, 8, 4
TOK, WIDE, HALF, D = 512, 256, 1024, 2048
POLES, UNITS = 80, 24
HI = TOK
LO = TOK + POLES
ROWS = TOK + 2 * POLES
NT = (((1,), (1,)), ((), ()))
NN = (((1,), (0,)), ((), ()))
OFFSETS = (0, -1, 1, 2)


def split(value):
    high = value.astype(BF16)
    return high, (value - high.astype(F32)).astype(BF16)


def mm(a, b, dims=NN):
    return lax.dot_general(a, b, dims, preferred_element_type=F32)


def minus_expm1_neg(u):
    series = jnp.ones_like(u)
    for n in range(9, 1, -1):
        series = 1.0 - u * (1.0 / n) * series
    return jnp.where(u < 0.25, u * series, 1.0 - jnp.exp(-u))


def kernel(
    g_hbm, m_hbm, rates_hbm, coeffs_hbm, out_ref,
    g_ref, rates_ref, coeffs_ref, grads, mats, kern_hi, kern_lo, proj_hi, proj_lo, parts, arrived, edge_hi, edge_lo,
    state_hi, state_lo, coef_col, rates_row, coef_row, rates_col, unit_rates, unit_out, unit_in,
    total_out, total_in, enter_out, enter_in,
    p1_send, p1_recv, p2_send, p2_recv, rl_send, rl_recv, sh_send, sh_recv,
    g_send, g_recv, m_send, m_recv, ms_send, ms_recv, u_send, u_recv,
    t_send, t_recv, e_send, e_recv, o_send, o_recv, l_sem, i_sem, near_sem,
):
    ctx, grp = lax.axis_index("ctx"), lax.axis_index("grp")
    x, z, y, c = ctx // NZ, ctx % NZ, grp // 2, grp % 2

    def device(x_to=None, z_to=None, y_to=None, c_to=None):
        pick = lambda new, own: own if new is None else new
        return (pick(x_to, x) * NZ + pick(z_to, z), pick(y_to, y) * 2 + pick(c_to, c))

    def remote(src, dst, send, recv, target):
        copy = pltpu.make_async_remote_copy(
            src_ref=src, dst_ref=dst, send_sem=send, recv_sem=recv,
            device_id=target, device_id_type=MESH,
        )
        return copy

    sibling = device(c_to=1 - c)
    slot = lambda x_of: (x_of + 4 - 2 * c) % NX
    col = lambda y_of: pl.ds(pl.multiple_of(c * HALF + y_of * WIDE, WIDE), WIDE)
    side = pl.ds(pl.multiple_of(c * HALF, HALF), HALF)

    barrier = pltpu.get_barrier_semaphore()
    partners = [device(z_to=(z + d) % NZ) for d in (1, NZ - 1)]
    partners += [device(x_to=(x + d) % NX) for d in (1, NX - 1)]
    partners += [device(y_to=(y + d) % NY) for d in (1, NY - 1)]
    partners += [sibling]
    for target in partners:
        pl.semaphore_signal(barrier, inc=1, device_id=target, device_id_type=MESH)

    low = pl.ds(pl.multiple_of(64 * (z % 2), 64), 64)
    fetches = [
        pltpu.make_async_copy(rates_hbm, rates_ref, i_sem.at[0]),
        pltpu.make_async_copy(coeffs_hbm, coeffs_ref, i_sem.at[1]),
        pltpu.make_async_copy(g_hbm, g_ref, i_sem.at[2]),
    ]
    for c_of in range(2):
        for y_of in range(NY):
            to, at = (c_of * NY + y_of) * WIDE, (y_of * 2 + c_of) * WIDE
            fetches.append(
                pltpu.make_async_copy(
                    m_hbm.at[:, :, at : at + WIDE],
                    mats.at[z // 2, :, c, low, to : to + WIDE],
                    i_sem.at[3 + c_of * NY + y_of],
                )
            )
    for fetch in fetches:
        fetch.start()
    for fetch in fetches[0:3]:
        fetch.wait()
    own_copy = pltpu.make_async_copy(g_ref, grads.at[slot(x), 0:TOK, col(y)], l_sem.at[0])
    own_copy.start()

    rates_row[...] = jnp.zeros_like(rates_row)
    coef_row[...] = jnp.zeros_like(coef_row)
    rates_row[0:1, 0:POLES] = rates_ref[...]
    coef_row[:, 0:POLES] = coeffs_ref[...]
    rates_col[...] = jnp.broadcast_to(rates_row[0:1, :], (128, 128)).T
    gains = jnp.sqrt(minus_expm1_neg(2.0 * rates_row[0:1, :]))
    rates_c = rates_col[0:POLES, :]
    state = jnp.zeros((POLES, WIDE), F32)
    for part in range(4):
        pos = lax.broadcasted_iota(jnp.int32, (POLES, 128), 1).astype(F32) + 128.0 * part
        dec_hi, dec_lo = split(jnp.exp(-pos * rates_c))
        rows = g_ref[128 * part : 128 * part + 128, :]
        state = state + mm(dec_hi, rows) + mm(dec_lo, rows)
    for group in range(10):
        for half in range(2):
            unit_out[group * 2 + half] = state[8 * group : 8 * group + 8, 128 * half : 128 * half + 128]
            unit_rates[group * 2 + half] = rates_col[8 * group : 8 * group + 8, :]

    for fetch in fetches[3:]:
        fetch.wait()
    pl.semaphore_wait(barrier, len(partners))

    def piece(z_of, d, k, way):
        start, size = 64 * (z_of % 2), 64
        if d == 4:
            start, size = start + 16 * (1 - way), 32
        return mats.at[z_of // 2, k, c, pl.ds(pl.multiple_of(start, 32), size), :]

    m_wait, ms_wait = [], []

    def ring(d, k, way):
        z_of = (z + NZ - way * (d - 1)) % NZ
        ref = piece(z_of, d, k, way)
        i = ((d - 1) * 2 + k) * 2 + (way + 1) // 2
        copy = remote(ref, ref, m_send.at[i], m_recv.at[i], device(z_to=(z + NZ + way) % NZ))
        copy.start()
        m_wait.append(copy)
        return copy

    def arrive(copy, d, k, way):
        z_of = (z + NZ - way * d) % NZ
        ref = piece(z_of, d, k, way)
        i = ((d - 1) * 2 + k) * 2 + (way + 1) // 2
        copy.wait_recv()
        over = remote(ref, ref, ms_send.at[i], ms_recv.at[i], sibling)
        over.start()
        ms_wait.append(over)
        return over

    ring_copies, over_copies = {}, {}

    def event(d, k):
        for way in (1, -1):
            over_copies[d, k, way] = arrive(ring_copies[d, k, way], d, k, way)
            if d < 4:
                ring_copies[d + 1, k, way] = ring(d + 1, k, way)

    for way in (1, -1):
        ring_copies[1, 0, way] = ring(1, 0, way)
    for step in range(3):
        for d in (1, NZ - 1):
            pl.semaphore_signal(
                near_sem.at[step], inc=1, device_id=device(z_to=(z + d) % NZ), device_id_type=MESH
            )
        pl.semaphore_wait(near_sem.at[step], 2)
    unit_copies = []
    for d in range(1, NZ):
        to = (z + d) % NZ
        copy = remote(
            unit_out.at[pl.ds(3 * to, 3)], unit_in.at[z], u_send.at[d], u_recv.at[d], device(z_to=to)
        )
        copy.start()
        unit_copies.append(copy)

    g_wait, sent = [], []

    def send_g(i, j, src, dst, target):
        copy = remote(src, dst, g_send.at[i], g_recv.at[j], target)
        copy.start()
        g_wait.append(copy)

    north = lambda d: (y + NY + d) % NY
    east = lambda d: (x + NX + d) % NX
    to_y = lambda d: device(y_to=north(d))
    to_x = lambda d: device(x_to=east(d))

    hi_rows, lo_rows = pl.ds(HI, POLES), pl.ds(LO, POLES)

    def states_first():
        for d in range(1, 4):
            ref = grads.at[slot(x), hi_rows, col(y)]
            send_g(d - 1, d - 1, ref, ref, to_y(d))
            ref = grads.at[slot(x), lo_rows, col(y)]
            send_g(3 + d - 1, 3 + d - 1, ref, ref, to_x(d))

    def states_second():
        for copy in g_wait[0:6]:
            copy.wait_recv()
        ref, dst = grads.at[slot(x), hi_rows, side], grads.at[x % 2, hi_rows, side]
        for d in range(1, 4):
            send_g(6 + d - 1, 6 + 2 * (x % 2) + c, ref, dst, device(x_to=east(d), c_to=x // 2))
        hi_over = remote(ref, dst, g_send.at[9], g_recv.at[6 + 2 * (x % 2) + c], sibling)

        @pl.when(x // 2 != c)
        def _():
            hi_over.start()

        dst = grads.at[0:2, lo_rows, col(y)]
        away = grads.at[2:4, lo_rows, col(y)]
        for d in range(1, 4):
            send_g(9 + d, 10 + 2 * y + c, dst, dst, to_y(d))
            send_g(12 + d, 10 + 2 * y + c, away, dst, device(y_to=north(d), c_to=1 - c))
        send_g(16, 10 + 2 * y + c, away, dst, sibling)
        return hi_over

    def states_finish():
        ref = grads.at[0, hi_rows, side]
        for b in range(2):
            for c_of in range(2):

                @pl.when(jnp.logical_not(jnp.logical_and(2 * c + b == x, c_of == c)))
                def _():
                    remote(ref, ref, g_send.at[0], g_recv.at[6 + 2 * b + c_of], sibling).wait_recv()

        ref2 = grads.at[0:2, lo_rows, col(y)]
        for y_of in range(NY):
            for c_of in range(2):

                @pl.when(jnp.logical_not(jnp.logical_and(y_of == y, c_of == c)))
                def _():
                    remote(ref2, ref2, g_send.at[0], g_recv.at[10 + 2 * y_of + c_of], sibling).wait_recv()

    class Tokens:
        def __init__(self, n, row, y_first):
            self.n, self.y_first = n, y_first
            self.rows, self.first, self.last = pl.ds(row, 256), pl.ds(row, 128), pl.ds(row + 128, 128)
            self.src = g_ref.at[row : row + 256, :]
            self.hop1, self.hop2 = (to_y, to_x) if y_first else (to_x, to_y)
            self.p1, self.p2, self.shares = {}, {}, []

        def ref(self, d1, d2, rows, s=None):
            dx, dy = (d2, d1) if self.y_first else (d1, d2)
            return grads.at[slot(east(dx)) if s is None else s, rows, col(north(dy))]

        def copy(self, src, dst, i, target, first=True):
            send, recv = (p1_send, p1_recv) if first else (p2_send, p2_recv)
            copy = remote(src, dst, send.at[self.n, i], recv.at[self.n, i], target)
            copy.start()
            sent.append(copy)
            return copy

        def onward(self, j, src=None):
            ref = self.ref(OFFSETS[j], 0, self.rows)
            for way in (1, -1):
                self.p2[j, way] = self.copy(
                    ref if src is None else src, ref, 2 * j + (way + 1) // 2, self.hop2(way), False
                )

        def start(self):
            halves = ((self.first, self.src.at[0:128, :]), (self.last, self.src.at[128:256, :]))
            for i in range(2):
                for at, way in ((0, 1), (1, -1)):
                    rows, src = halves[i ^ at]
                    self.p1[at, i] = self.copy(src, self.ref(0, 0, rows), 2 * i + at, self.hop1(way))

        def mid(self):
            for i, way, rows in ((0, 1, self.first), (1, -1, self.last)):
                self.p1[i, 0].wait_recv()
                ref = self.ref(-way, 0, rows)
                self.p1[i, 2] = self.copy(ref, ref, i + 4, self.hop1(way))

        def opposite(self):
            self.p1[0, 2].wait_recv()
            self.p1[1, 2].wait_recv()
            self.onward(3)

        def relay(self, j):
            for way, rows in ((1, self.first), (-1, self.last)):
                self.p2[j, way].wait_recv()
                owner = east(-way) if self.y_first else east(OFFSETS[j])
                at = 8 * c + 2 * j + (way + 1) // 2 if self.y_first else 4 * c + 2 * (owner % 2) + (way + 1) // 2
                target = (
                    device(x_to=east(way), c_to=owner // 2)
                    if self.y_first
                    else device(y_to=north(way), c_to=owner // 2)
                )
                copy = remote(
                    self.ref(OFFSETS[j], -way, rows), self.ref(OFFSETS[j], -way, rows, owner % 2),
                    rl_send.at[self.n, 2 * j + (way + 1) // 2], rl_recv.at[self.n, at], target,
                )
                copy.start()
                sent.append(copy)

        def share_copy(self, i, src, dst):
            return remote(src, dst, sh_send.at[self.n, i], sh_recv.at[self.n, i], sibling)

        def share(self):
            if self.y_first:
                mine = x // 2 == 1 - c
                buddy = lambda v: v + 1 - 2 * (v % 2)
                s0 = slot(jnp.where(mine, x, buddy(east(2))))
                s1 = slot(jnp.where(mine, buddy(x), x))
                at = lambda s: grads.at[s, self.rows, side]
                copy = self.share_copy(0, at(s0), at(s0 - 2))
                copy.start()
                sent.append(copy)
                self.shares.append(copy)
                self.extra = self.share_copy(1, at(jnp.where(mine, s1, 2)), at(jnp.where(mine, s1 - 2, 0)))

                @pl.when(mine)
                def _():
                    self.extra.start()
            else:
                for i, dy in enumerate((0, -1, 1)):
                    at = lambda lo: grads.at[lo : lo + 2, self.rows, col(north(dy))]
                    copy = self.share_copy(i, at(2), at(0))
                    copy.start()
                    sent.append(copy)
                    self.shares.append(copy)

        def finish(self):
            for copy in self.shares:
                copy.wait_recv()
            piece_ref = grads.at[0, self.first, 0:WIDE]

            def wait_relays(count):
                for at in range(count):
                    remote(
                        piece_ref, piece_ref, rl_send.at[self.n, 0], rl_recv.at[self.n, at], sibling
                    ).wait_recv()

            if self.y_first:

                @pl.when(x // 2 == c)
                def _():
                    self.extra.wait_recv()

                @pl.when(east(2) // 2 == c)
                def _():
                    wait_relays(16)
            else:
                wait_relays(8)

        def drain(self):
            if self.y_first:

                @pl.when(x // 2 == 1 - c)
                def _():
                    self.extra.wait_send()

    tok_a, tok_b = Tokens(0, 0, True), Tokens(1, 256, False)

    tok_a.start()
    tok_b.start()

    tok_a.onward(0, tok_a.src)
    tok_b.onward(0, tok_b.src)
    for way in (1, -1):
        ring_copies[1, 1, way] = ring(1, 1, way)
    own_ref = mats.at[z // 2, :, c, low, :]
    own_over = remote(own_ref, own_ref, ms_send.at[16], ms_recv.at[16], sibling)
    own_over.start()

    own_units = pl.ds(3 * z, 3)
    total_copies, enter_copies = [], []

    def hand_on():
        lam = jnp.exp(-float(TOK) * unit_rates[own_units])
        unit_in[z] = unit_out[own_units]
        for copy in unit_copies:
            copy.wait_recv()
        run = jnp.zeros((3, 8, 128), F32)
        for z_of in range(NZ - 1, -1, -1):
            enter_out[z_of] = run
            run = unit_in[z_of] + lam * run
        total_out[...] = run
        total_in[x] = run
        for d in range(1, NX):
            copy = remote(
                total_out, total_in.at[x], t_send.at[d], t_recv.at[d], device(x_to=(x + d) % NX)
            )
            copy.start()
            total_copies.append(copy)

    def send_enter():
        for copy in total_copies:
            copy.wait_recv()
        lam_row = jnp.exp(-float(TOK * NZ) * unit_rates[own_units])
        carry = jnp.zeros((3, 8, 128), F32)
        for x_of in range(NX - 1, 0, -1):
            carry = jnp.where(x_of > x, total_in[x_of] + lam_row * carry, carry)
        lam = jnp.exp(-float(TOK) * unit_rates[own_units])
        for z_of in range(NZ - 1, -1, -1):
            enter_out[z_of] = enter_out[z_of] + carry
            carry = lam * carry
        for d in range(1, NZ):
            to = (z + d) % NZ
            copy = remote(
                enter_out.at[to], enter_in.at[own_units], e_send.at[d], e_recv.at[d], device(z_to=to)
            )
            copy.start()
            enter_copies.append(copy)
        enter_in[own_units] = enter_out[z]

    def store_enter():
        for d in range(1, NZ):
            source = (z + NZ - d) % NZ
            remote(
                enter_out.at[0], enter_in.at[pl.ds(3 * source, 3)], e_send.at[d], e_recv.at[d], sibling
            ).wait_recv()
        for group in range(10):
            for half in range(2):
                high, rest = split(enter_in[group * 2 + half])
                grads_cols = pl.ds(pl.multiple_of(c * HALF + y * WIDE + 128 * half, 128), 128)
                grads[slot(x), HI + 8 * group : HI + 8 * group + 8, grads_cols] = high
                grads[slot(x), LO + 8 * group : LO + 8 * group + 8, grads_cols] = rest

    rates_r = rates_row[0:1, :]
    rise_pos = lax.broadcasted_iota(jnp.int32, (TOK, 128), 0).astype(F32)
    falling = jnp.exp((rise_pos - 256.0) * rates_r)
    rising = jnp.exp((256.0 - rise_pos) * rates_r)
    edge = gains * jnp.exp((rise_pos - float(TOK)) * rates_r)
    edge_hi[...], edge_lo[...] = split(edge)

    def taps(th, k):
        size = 256 * (th + 1)
        scaled = rising[256 * th : 256 * th + 256] * (coef_row[pl.ds(4 * y + k, 1), :] * gains)
        mat = lax.dot_general(
            falling[0:size], scaled, NT, precision=lax.Precision.HIGHEST, preferred_element_type=F32
        )
        s_at = lax.broadcasted_iota(jnp.int32, (size, 256), 0)
        t_at = lax.broadcasted_iota(jnp.int32, (size, 256), 1) + 256 * th
        high, rest = split(jnp.where(t_at >= s_at, mat, 0.0))
        at = (k % 2) * HALF + th * TOK + (k // 2) * 256
        kern_hi[0:size, at : at + 256] = high
        kern_lo[0:size, at : at + 256] = rest

    def more_taps(ks):
        for k in ks:
            taps(1, k)
            coef_col[k] = jnp.broadcast_to(coef_row[pl.ds(4 * y + k, 1), :], (128, 128)).T

    tok_a.mid()
    tok_b.mid()
    hand_on()
    for j in (1, 2):
        tok_a.p1[j - 1, 1].wait_recv()
        tok_a.onward(j)
        tok_b.p1[j - 1, 1].wait_recv()
        tok_b.onward(j)
    for k in range(4):
        taps(0, k)
    own_copy.wait()
    tok_a.opposite()
    tok_b.opposite()
    send_enter()
    event(1, 0)
    tok_a.relay(0)
    tok_b.relay(0)
    more_taps((0, 1))
    tok_a.relay(1)
    tok_b.relay(1)
    event(1, 1)
    tok_a.relay(2)
    tok_b.relay(2)
    state_hi[...] = jnp.zeros_like(state_hi)
    state_lo[...] = jnp.zeros_like(state_lo)
    store_enter()
    tok_a.relay(3)
    tok_b.relay(3)
    states_first()
    tok_a.share()
    tok_b.share()
    more_taps((2,))
    event(2, 0)
    more_taps((3,))

    def project(q, kk, ths=(0, 1)):
        weights = mats[q, kk].reshape(256, D)
        parts_of = [(block, th) for block in range(2) for th in ths]
        tiles = [mm(grads[block, 256 * th : 256 * th + 256, :], weights, NT) for block, th in parts_of]
        for (block, th), tile in zip(parts_of, tiles):
            high, rest = split(tile)
            for c_of in range(2):
                at = kk * HALF + th * TOK + c_of * 256
                lanes, own = slice(128 * block, 128 * block + 128), slice(128 * c_of, 128 * c_of + 128)
                proj_hi[at : at + 256, lanes] = high[:, own]
                proj_lo[at : at + 256, lanes] = rest[:, own]

    def near(sh, kk):
        s_rows = slice(256 * sh, 256 * sh + 256)
        t_rows = slice(HALF * kk + TOK * sh, HALF * kk + HALF)
        return (
            mm(kern_hi[s_rows, t_rows], proj_hi[t_rows, :])
            + mm(kern_hi[s_rows, t_rows], proj_lo[t_rows, :])
            + mm(kern_lo[s_rows, t_rows], proj_hi[t_rows, :])
        )

    def enter(q):
        both = mm(grads[0:2, HI:ROWS, :].reshape(4 * POLES, D), mats[q].reshape(512, D), NT)
        for block in range(2):
            total = jnp.zeros((POLES, 128), F32)
            top = 2 * POLES * block
            for kk in range(2):
                for c_of in range(2):
                    at = 256 * kk + 128 * c_of
                    lanes = slice(at, at + 128)
                    total = total + coef_col[2 * c_of + kk, 0:POLES, :] * (
                        both[top : top + POLES, lanes] + both[top + POLES : top + 2 * POLES, lanes]
                    )
            high, rest = split(total)
            state_hi[0:POLES, 128 * block : 128 * block + 128] = high
            state_lo[0:POLES, 128 * block : 128 * block + 128] = rest

    def far(sh):
        s_rows = slice(256 * sh, 256 * sh + 256)
        return (
            mm(edge_hi[s_rows, :], state_hi[...])
            + mm(edge_hi[s_rows, :], state_lo[...])
            + mm(edge_lo[s_rows, :], state_hi[...])
        )

    out_waits = []

    def deliver(n, q, sh):
        s_rows = slice(256 * sh, 256 * sh + 256)
        for block in range(2):
            own = jnp.logical_and(jnp.logical_and(2 * c + block == x, x == y), q // 2 == c)
            cols = pl.ds(pl.multiple_of((q % 2) * 128, 128), 128)
            src, dst = parts.at[n, block, s_rows, :], arrived.at[y, s_rows, cols]
            done = o_recv.at[y, 2 * (q % 2) + sh]
            away = remote(
                src, dst, o_send.at[4 * n + 2 * block + sh], done,
                device(x_to=2 * c + block, y_to=x, c_to=q // 2),
            )
            local = pltpu.make_async_copy(src, dst, done)

            @pl.when(jnp.logical_not(own))
            def _():
                away.start()

            @pl.when(own)
            def _():
                local.start()

            out_waits.append((own, away))

    def store(n, sh, value, add=False):
        s_rows = slice(256 * sh, 256 * sh + 256)
        for block in range(2):
            new = value[:, 128 * block : 128 * block + 128]
            parts[n, block, s_rows, :] = parts[n, block, s_rows, :] + new if add else new

    def over_in(d, k):
        for way in (1, -1):
            if (d, k, way) in over_copies:
                over_copies[d, k, way].wait_recv()

    q_own = z // 2
    lean = 1 - 2 * (z % 2)
    order = [q_own, (q_own + 4 - lean) % 4, (q_own + 4 + lean) % 4, (q_own + 2) % 4]

    own_over.wait_recv()
    over_in(1, 0)
    over_in(1, 1)
    hi_over = states_second()
    tok_a.finish()
    tok_b.finish()
    project(order[0], 0)
    project(order[0], 1)
    event(2, 1)
    for sh in range(2):
        store(0, sh, near(sh, 0) + near(sh, 1))
    over_in(2, 0)
    over_in(2, 1)
    project(order[1], 0)
    event(3, 0)
    project(order[1], 1)
    states_finish()
    enter(order[0])
    for sh in range(2):
        store(0, sh, far(sh), True)
        deliver(0, order[0], sh)
    enter(order[1])
    for sh in (1, 0):
        store(1, sh, near(sh, 0) + near(sh, 1) + far(sh))
        deliver(1, order[1], sh)
    event(3, 1)
    over_in(3, 0)
    project(order[2], 0)
    for sh in range(2):
        store(2, sh, near(sh, 0))
    event(4, 0)
    over_in(3, 1)
    project(order[2], 1)
    enter(order[2])
    for sh in (1, 0):
        store(2, sh, near(sh, 1) + far(sh), True)
        deliver(2, order[2], sh)
    event(4, 1)
    over_in(4, 0)
    project(order[3], 0)
    for sh in range(2):
        store(3, sh, near(sh, 0))
    over_in(4, 1)
    enter(order[3])
    for sh in (1, 0):
        project(order[3], 1, (sh,))
        store(3, sh, near(sh, 1) + far(sh), True)
        deliver(3, order[3], sh)

    for n in range(4):
        q = order[n]

        @pl.when(q // 2 == c)
        def _():
            cols = pl.ds(pl.multiple_of((q % 2) * 128, 128), 128)
            for sh in (1, 0):
                s_rows = slice(256 * sh, 256 * sh + 256)
                for y_of in range(NY):
                    ref = arrived.at[y_of, s_rows, cols]
                    pltpu.make_async_copy(ref, ref, o_recv.at[y_of, 2 * (q % 2) + sh]).wait()
                total = arrived[0, s_rows, cols] + arrived[1, s_rows, cols]
                total = total + arrived[2, s_rows, cols] + arrived[3, s_rows, cols]
                out_ref[s_rows, cols] = total.astype(BF16)

    tok_a.drain()

    @pl.when(x // 2 != c)
    def _():
        hi_over.wait_send()

    for copy in unit_copies + total_copies + enter_copies + m_wait + ms_wait + g_wait + sent + [own_over]:
        copy.wait_send()
    for own, away in out_waits:

        @pl.when(jnp.logical_not(own))
        def _():
            away.wait_send()


def per_device(out_grad, filter_mats, coeffs, pole_rates):
    held = (out_grad, filter_mats, pole_rates.reshape(1, POLES), coeffs)
    dma = pltpu.SemaphoreType.DMA
    vmem = pl.BlockSpec(memory_space=pltpu.VMEM)
    return pl.pallas_call(
        kernel,
        out_shape=jax.ShapeDtypeStruct((TOK, WIDE), BF16),
        in_specs=[pl.BlockSpec(memory_space=pltpu.MemorySpace.HBM)] * 4,
        out_specs=vmem,
        scratch_shapes=[
            pltpu.VMEM((TOK, WIDE), BF16),
            pltpu.VMEM((1, POLES), F32),
            pltpu.VMEM((16, POLES), F32),
            pltpu.VMEM((NX, ROWS, D), BF16),
            pltpu.VMEM((4, 2, 2, 128, D), BF16),
            pltpu.VMEM((TOK, D), BF16),
            pltpu.VMEM((TOK, D), BF16),
            pltpu.VMEM((D, 256), BF16),
            pltpu.VMEM((D, 256), BF16),
            pltpu.VMEM((4, 2, TOK, 128), F32),
            pltpu.VMEM((NY, TOK, WIDE), F32),
            pltpu.VMEM((TOK, 128), BF16),
            pltpu.VMEM((TOK, 128), BF16),
            pltpu.VMEM((128, 256), BF16),
            pltpu.VMEM((128, 256), BF16),
            pltpu.VMEM((4, 128, 128), F32),
            pltpu.VMEM((8, 128), F32),
            pltpu.VMEM((16, 128), F32),
            pltpu.VMEM((128, 128), F32),
            pltpu.VMEM((UNITS, 8, 128), F32),
            pltpu.VMEM((UNITS, 8, 128), F32),
            pltpu.VMEM((NZ, 3, 8, 128), F32),
            pltpu.VMEM((3, 8, 128), F32),
            pltpu.VMEM((NX, 3, 8, 128), F32),
            pltpu.VMEM((NZ, 3, 8, 128), F32),
            pltpu.VMEM((UNITS, 8, 128), F32),
            dma((2, 6)), dma((2, 6)), dma((2, 8)), dma((2, 8)),
            dma((2, 8)), dma((2, 16)), dma((2, 3)), dma((2, 3)),
            dma((17,)), dma((18,)),
            dma((16,)), dma((16,)), dma((17,)), dma((17,)),
            dma((NZ,)), dma((NZ,)), dma((NX,)), dma((NX,)), dma((NZ,)), dma((NZ,)),
            dma((16,)), dma((NY, 4)), dma((1,)), dma((11,)), pltpu.SemaphoreType.REGULAR((3,)),
        ],
        compiler_params=pltpu.CompilerParams(
            collective_id=0, has_side_effects=True, vmem_limit_bytes=44 * 1024 * 1024
        ),
        name="spectral_grad",
    )(*[pltpu.with_memory_space_constraint(v, pltpu.MemorySpace.HBM) for v in held])


def solution(mesh):
    placed = (P("ctx", "grp"), P("grp", "ctx", None), P(), P())
    return jax.shard_map(
        per_device, mesh=mesh, in_specs=placed, out_specs=P("ctx", "grp"), check_vma=False
    )
```
